512 devices in a mesh: dp: 16 (over z), fsdp: 32 (over x, y, core).
Axes of the slice: x: 4, y: 4, z: 16, core: 2. Of those that a mesh axis runs over, the one named last changes fastest.
Arguments:
- txt_tokens: bfloat16 [512, 8, 3072], P(('dp', 'fsdp')), may hold values from -6 to 6
- concept_table: bfloat16 [4096, 3072], P('dp'), may hold values from -6 to 6
- concept_ids: int32 [512], P(('dp', 'fsdp')), may hold values from 0 to 4095
- positions: int32 [512], P(('dp', 'fsdp')), may hold values from 0 to 7
- timesteps: int32 [512], P(('dp', 'fsdp')), may hold values from 0 to 63
- counts: int32 [4096], P('dp'), may hold values from 1 to 16
- mod_table: bfloat16 [64, 2, 3072], P(None, None, 'fsdp'), may hold values from -1.5 to 1.5
- kv_weight: bfloat16 [3072, 3072], P('fsdp'), may hold values from -0.109375 to 0.109375
- kv_bias: float32 [3072], replicated, may hold values from -3 to 3
- key_gain: float32 [128], replicated, may hold values from 0.5 to 1.5
- img_query: bfloat16 [512, 192, 1536], P(('dp', 'fsdp')), may hold values from -256 to 256
- img_key: bfloat16 [512, 192, 1536], P(('dp', 'fsdp')), may hold values from -6 to 6
- img_value: bfloat16 [512, 192, 1536], P(('dp', 'fsdp')), may hold values from -6 to 6
- out_grad: bfloat16 [512, 192, 1536], P(('dp', 'fsdp')), may hold values from -6 to 6
Outputs:
- table_grad: float32 [4096, 3072], P('dp', 'fsdp')
The draws below stay inside these ranges and needn't reach their ends.
Inputs may be any that keep to these rules, and one draw needn't show every extreme that they name: `concept_ids`: concept of each sample, some concepts far more common than others.
All inputs are finite; a program needn't handle non-finite values.
Results may differ from the reference program's by a relative error of at most 0.0083.
Values may be sent and summed in bfloat16 or wider, within the bound.
A program may use at most 64 MiB of HBM per device.

```python
import math
import jax
import jax.numpy as jnp
import numpy as np
from jax import lax

D = 3072
HEADS = 12
DH = 128
HW = 1536
LT = 8
LI = 192
NT = 64
CONCEPTS = 4096
SAMPLES = 512


def draw_pair(key):
    shape = (SAMPLES, LI, HEADS * DH)
    keys_v = jnp.clip(jax.random.normal(jax.random.fold_in(key, 101), shape, jnp.float32), -6.0, 6.0)
    query_v = jnp.clip(jax.random.normal(jax.random.fold_in(key, 202), shape, jnp.float32), -6.0, 6.0)
    return (query_v, keys_v)


def draw_img_query(key, part):
    return draw_pair(key)[0].astype(jnp.bfloat16)


def draw_img_key(key, part):
    return draw_pair(key)[1].astype(jnp.bfloat16)


def with_ends(drawn, rng, smallest, high):
    dims = drawn.shape
    index_at = [jax.random.randint(jax.random.fold_in(rng, axis), (), 0, dims[axis]) for axis in range(len(dims))]
    drawn = drawn.at[tuple(index_at)].set(smallest)
    longest = dims.index(max(dims))
    index_at[longest] = (index_at[longest] + 1) % dims[longest]
    return drawn.at[tuple(index_at)].set(high)


def block_levels(stream_key, extent, split, low, largest):
    gain, own = 1.0, jax.random.fold_in(stream_key, 6)
    for axis_at, parts in split:
        draws = jnp.exp(jax.random.uniform(jax.random.fold_in(own, axis_at), (parts,), jnp.float32, low / len(split), largest / len(split)))
        gain = gain * jnp.repeat(draws, extent[axis_at] // parts).reshape([-1 if axis == axis_at else 1 for axis in range(len(extent))])
    return gain


def rank_bounds(amount, lean):
    portions = [(1 << 20) // math.isqrt(rank ** lean) + 1 for rank in range(1, amount + 1)]
    scale = 1 + sum(portions) // (1 << 30)
    return np.cumsum(np.array([max(1, weight // scale) for weight in portions]))


def skewed_ids(rng, dims, amount, skew):
    grid = rank_bounds(amount, skew)
    lot = jax.random.randint(jax.random.fold_in(rng, 1), dims, 0, int(grid[amount - 1]))
    grade = jnp.searchsorted(jnp.asarray(grid, jnp.int32), lot, side="right")
    return jax.random.permutation(jax.random.fold_in(rng, 2), amount)[grade].astype(jnp.int32)


def scatter_about(own_key, shape, width, limit, pieces=(), held_as=jnp.bfloat16):
    values = width * jax.random.normal(own_key, shape, jnp.float32)
    if pieces:
        values = values * block_levels(own_key, shape, pieces, -0.22, 0.18)
    return jnp.clip(values, -limit, limit).astype(held_as)


def setup_inputs(seed: int = 0) -> dict:
    splits = jax.random.split(jax.random.key(seed), 15)
    txt_tokens = scatter_about(splits[0], (SAMPLES, LT, D), 1.0, 6.0, ((0, 512),))
    concept_table = scatter_about(splits[1], (CONCEPTS, D), 1.0, 6.0, ((0, 16),))
    concept_ids = with_ends(skewed_ids(splits[2], (SAMPLES,), CONCEPTS, 2), jax.random.fold_in(splits[2], 3), 0, CONCEPTS - 1).astype(jnp.int32)
    positions = with_ends(jax.random.randint(splits[3], (SAMPLES,), 0, LT), jax.random.fold_in(splits[3], 1), 0, LT - 1).astype(jnp.int32)
    timesteps = with_ends(jax.random.randint(splits[4], (SAMPLES,), 0, NT), jax.random.fold_in(splits[4], 1), 0, NT - 1).astype(jnp.int32)
    counts = with_ends(jax.random.randint(splits[5], (CONCEPTS,), 1, 17), jax.random.fold_in(splits[5], 1), 1, 16).astype(jnp.int32)
    mod_table = scatter_about(splits[6], (NT, 2, D), 0.3, 1.5, ((2, 32),))
    kv_weight = scatter_about(splits[7], (D, 2 * HW), D ** -0.5, 0.109375, ((0, 32),))
    kv_bias = scatter_about(splits[8], (2 * HW,), 0.5, 3.0, (), jnp.float32)
    key_gain = jnp.clip(1.0 + 0.1 * jax.random.normal(splits[9], (DH,), jnp.float32), 0.5, 1.5)
    img_query = draw_img_query(jax.random.fold_in(splits[14], 71), 0)
    img_key = draw_img_key(jax.random.fold_in(splits[14], 71), 0)
    img_value = scatter_about(splits[12], (SAMPLES, LI, HW), 1.0, 6.0, ((0, 512),))
    out_grad = scatter_about(splits[13], (SAMPLES, LI, HW), 1.0, 6.0, ((0, 512),))
    return dict(txt_tokens=txt_tokens, concept_table=concept_table, concept_ids=concept_ids, positions=positions, timesteps=timesteps, counts=counts, mod_table=mod_table, kv_weight=kv_weight, kv_bias=kv_bias, key_gain=key_gain, img_query=img_query, img_key=img_key, img_value=img_value, out_grad=out_grad)


EPSILON = 1e-06

def layer_norm(values):
    centre = lax.optimization_barrier(jnp.mean(values, -1, keepdims=True))
    spread = lax.optimization_barrier(jnp.mean((values - centre) ** 2, -1, keepdims=True))
    inverse = lax.rsqrt(spread + EPSILON)
    return ((values - centre) * inverse, inverse[..., 0])

def reference(txt_tokens, concept_table, concept_ids, positions, timesteps, counts, mod_table, kv_weight, kv_bias, key_gain, img_query, img_key, img_value, out_grad):
    table_hat, table_rstd = layer_norm(concept_table.astype(jnp.float32))
    table_hat = table_hat.astype(jnp.bfloat16)
    weight_f = kv_weight.astype(jnp.float32)
    root_dh = jnp.sqrt(jnp.float32(DH))

    def one_sample(packed):
        tokens, concept, place, bucket, queries, img_keys, img_vals, grad_out = packed
        own_hat = layer_norm(tokens.astype(jnp.float32))[0].astype(jnp.bfloat16)
        concept_row = lax.dynamic_index_in_dim(table_hat, concept, 0, keepdims=False)
        is_place = (jnp.arange(LT, dtype=jnp.int32) == place)[:, None]
        normed = jnp.where(is_place, concept_row[None, :], own_hat)
        modul = lax.dynamic_index_in_dim(mod_table, bucket, 0, keepdims=False).astype(jnp.float32)
        shift_row = modul[0]
        scale_row = 1.0 + modul[1]
        modulated = (scale_row * normed.astype(jnp.float32) + shift_row).astype(jnp.bfloat16)
        kv_rows = jnp.dot(modulated, kv_weight, preferred_element_type=jnp.float32) + kv_bias
        key_raw = kv_rows[:, :HW].reshape(LT, HEADS, DH)
        key_inv = lax.rsqrt(lax.optimization_barrier(jnp.mean(key_raw * key_raw, -1)) + EPSILON)
        key_norm = (key_raw * key_inv[..., None] * key_gain).astype(jnp.bfloat16).reshape(LT, HW)
        val_txt = kv_rows[:, HW:].astype(jnp.bfloat16)
        keys_all = jnp.concatenate([key_norm, img_keys], 0).astype(jnp.float32).reshape(LT + LI, HEADS, DH)
        vals_all = jnp.concatenate([val_txt, img_vals], 0).astype(jnp.float32).reshape(LT + LI, HEADS, DH)
        query_f = queries.astype(jnp.float32).reshape(LI, HEADS, DH)
        scores = jnp.einsum('qhd,khd->hqk', query_f, keys_all) / root_dh
        row_top = lax.optimization_barrier(jnp.max(scores, -1, keepdims=True))
        raised = jnp.exp(scores - row_top)
        prob_full = raised / lax.optimization_barrier(jnp.sum(raised, -1, keepdims=True))
        prob_low = lax.optimization_barrier(prob_full.astype(jnp.bfloat16))
        attended = jnp.einsum('hqk,khd->qhd', prob_low.astype(jnp.float32), vals_all)
        grad_f = grad_out.astype(jnp.float32).reshape(LI, HEADS, DH)
        row_delta = jnp.einsum('qhd,qhd->hq', grad_f, attended)
        prob_pos = lax.dynamic_index_in_dim(prob_full, place, 2, keepdims=False)
        val_pos = lax.dynamic_index_in_dim(vals_all, place, 0, keepdims=False)
        grad_prob = jnp.einsum('qhd,hd->hq', grad_f, val_pos)
        grad_score = prob_pos * (grad_prob - row_delta)
        grad_val = jnp.einsum('hq,qhd->hd', prob_pos, grad_f)
        grad_key = jnp.einsum('hq,qhd->hd', grad_score, query_f) / root_dh
        raw_pos = lax.dynamic_index_in_dim(key_raw, place, 0, keepdims=False)
        inv_pos = lax.dynamic_index_in_dim(key_inv, place, 0, keepdims=False)
        normed_key = raw_pos * inv_pos[:, None]
        grad_norm = grad_key * key_gain
        grad_raw = inv_pos[:, None] * (grad_norm - normed_key * lax.optimization_barrier(jnp.mean(grad_norm * normed_key, -1, keepdims=True)))
        grad_kv = jnp.concatenate([grad_raw.reshape(HW), grad_val.reshape(HW)])
        grad_mod = jnp.dot(weight_f, grad_kv, precision=lax.Precision.HIGHEST) * scale_row
        concept_f = concept_row.astype(jnp.float32)
        return grad_mod - jnp.mean(grad_mod) - concept_f * jnp.mean(grad_mod * concept_f)
    row_grad = lax.map(one_sample, (txt_tokens, concept_ids, positions, timesteps, img_query, img_key, img_value, out_grad))
    summed = jax.ops.segment_sum(row_grad, concept_ids, num_segments=CONCEPTS)
    return summed * (table_rstd / counts.astype(jnp.float32))[:, None]
```

```python
import functools
import jax
import jax.numpy as jnp
from jax import lax
from jax.experimental import pallas as pl
from jax.experimental.pallas import tpu as pltpu
from jax.sharding import PartitionSpec as P

EPSILON = 1e-06
LANES = 128
BF = jnp.bfloat16
F32 = jnp.float32
MESH = pl.DeviceIdType.MESH
NT_DIMS = (((1,), (1,)), ((), ()))
TN_DIMS = (((0,), (0,)), ((), ()))


def split_two(values):
    high = values.astype(BF)
    low = (values - high.astype(F32)).astype(BF)
    return high, low


def iota(shape, axis):
    return lax.broadcasted_iota(jnp.int32, shape, axis)


def step_kernel(
    dims,
    ids_s,
    pos_s,
    time_s,
    tok,
    table,
    counts,
    modp,
    weight,
    bias,
    gain,
    q_any,
    k_any,
    v_any,
    g_any,
    out,
    q,
    k,
    v,
    g,
    id_buf,
    id_own,
    row32,
    row_send,
    row_recv,
    c32,
    c_row,
    tok_msg,
    tok_recv,
    w_recv,
    mod_recv,
    mod_all,
    part,
    part_recv,
    side,
    side_recv,
    kv,
    m_img,
    l_img,
    d_img,
    dkv32,
    raw32,
    s1_32,
    s2_32,
    dkv_own,
    dkv_recv,
    dkv_wide,
    g_own,
    g_recv,
    load_sem,
    send_sem,
    recv_sem,
):
    zs, ns, m = dims
    z = lax.axis_index("dp")
    f = lax.axis_index("fsdp")
    groups = ns // m
    r = lax.rem(f, m)
    grp = lax.div(f, m)
    tok_len, width = tok.shape
    slice_w = weight.shape[0]
    kv_w = weight.shape[1]
    head_w = kv_w // 2
    heads = head_w // LANES
    block = kv_w // m
    group_w = slice_w * m
    n_img = q.shape[0]
    rows_own = table.shape[0]
    buckets = modp.shape[0] // 2
    inv_root = 1.0 / (LANES**0.5)

    loads = [
        pltpu.make_async_copy(src, dst, load_sem.at[i])
        for i, (src, dst) in enumerate(((q_any, q), (k_any, k), (v_any, v), (g_any, g)))
    ]
    for copy in loads:
        copy.start()

    barrier = pltpu.get_barrier_semaphore()

    def greet_plane(j, c):
        pl.semaphore_signal(
            barrier, inc=1, device_id=(z, lax.rem(f + j, ns)), device_id_type=MESH
        )
        return c

    def greet_line(j, c):
        pl.semaphore_signal(
            barrier, inc=1, device_id=(lax.rem(z + j, zs), f), device_id_type=MESH
        )
        return c

    lax.fori_loop(1, zs, greet_line, 0)
    lax.fori_loop(1, ns, greet_plane, 0)

    own_id = ids_s[0]
    own_pos = pos_s[0]
    own_time = time_s[0]
    id_own[...] = jnp.full(id_own.shape, own_id, jnp.int32)
    id_buf[z] = id_own[...]
    w_recv[pl.ds(pl.multiple_of(r * slice_w, 16), slice_w), :] = weight[
        :, pl.ds(pl.multiple_of(r * block, LANES), block)
    ]
    mod_recv[r] = modp[...]

    pl.semaphore_wait(barrier, zs - 1 + ns - 1)

    def remote(src, dst, phase, device):
        return pltpu.make_async_remote_copy(
            src_ref=src,
            dst_ref=dst,
            send_sem=send_sem.at[phase],
            recv_sem=recv_sem.at[phase],
            device_id=device,
            device_id_type=MESH,
        )

    def finish(ref, phase):
        pltpu.make_async_copy(ref, ref, recv_sem.at[phase]).wait()

    def drain(ref, phase):
        pltpu.make_async_copy(ref, ref, send_sem.at[phase]).wait()

    def send_id(j, c):
        remote(id_own, id_buf.at[z], 0, (lax.rem(z + j, zs), f)).start()
        return c

    lax.fori_loop(1, zs, send_id, 0)

    def send_weight(j, c):
        peer = lax.rem(r + j, m)
        device = (z, grp * m + peer)
        remote(
            weight.at[:, pl.ds(pl.multiple_of(peer * block, LANES), block)],
            w_recv.at[pl.ds(pl.multiple_of(r * slice_w, 16), slice_w), :],
            1,
            device,
        ).start()
        remote(modp, mod_recv.at[r], 2, device).start()
        return c

    lax.fori_loop(1, m, send_weight, 0)

    for copy in loads:
        copy.wait()

    def image_head(h, c):
        lanes = pl.ds(pl.multiple_of(h * LANES, LANES), LANES)
        scores = (
            lax.dot_general(k[:, lanes], q[:, lanes], NT_DIMS, preferred_element_type=F32)
            * inv_root
        )
        grads = lax.dot_general(v[:, lanes], g[:, lanes], NT_DIMS, preferred_element_type=F32)
        top = jnp.max(scores, 0, keepdims=True)
        raised = jnp.exp(scores - top)
        m_img[h] = top
        l_img[h] = jnp.sum(raised, 0, keepdims=True)
        d_img[h] = jnp.sum(raised.astype(BF).astype(F32) * grads, 0, keepdims=True)
        return c

    half = heads // 2
    lax.fori_loop(0, half, image_head, 0)

    tok_f = tok[...].astype(F32)
    centre = jnp.mean(tok_f, -1, keepdims=True)
    spread = jnp.mean((tok_f - centre) ** 2, -1, keepdims=True)
    tok_hat = ((tok_f - centre) * lax.rsqrt(spread + EPSILON)).astype(BF).astype(F32)

    finish(id_buf.at[pl.ds(0, zs - 1)], 0)
    wanted = id_buf[:, 0, :][:, :1]
    pick = (iota((zs, rows_own), 1) + z * rows_own == wanted).astype(F32).astype(BF)
    rows = jnp.dot(pick, table[...], preferred_element_type=F32)
    for c in range(width // LANES):
        row32[:, c, :] = rows[:, c * LANES : (c + 1) * LANES]
    row_send[...] = row32[...].astype(BF)
    row_recv[z] = row_send[z]

    def send_row(j, c):
        peer = lax.rem(z + j, zs)
        remote(row_send.at[peer], row_recv.at[z], 3, (peer, f)).start()
        return c

    lax.fori_loop(1, zs, send_row, 0)

    lax.fori_loop(half, heads, image_head, 0)

    finish(mod_recv.at[pl.ds(0, m - 1)], 2)
    lane_row = iota((LANES, group_w), 0)
    lane_col = iota((LANES, group_w), 1)
    mods = jnp.zeros((2 * buckets, group_w), F32)
    for c in range(m):
        place = ((lane_col == lane_row + c * slice_w) & (lane_row < slice_w)).astype(F32)
        mods += jnp.dot(mod_recv[c], place.astype(BF), preferred_element_type=F32)
    mod_all[...] = mods.astype(BF)

    table_f = table[...].astype(F32)
    t_centre = jnp.mean(table_f, -1, keepdims=True)
    t_spread = jnp.mean((table_f - t_centre) ** 2, -1, keepdims=True)
    t_rstd = lax.rsqrt(t_spread + EPSILON)
    diag = iota((rows_own, rows_own), 0) == iota((rows_own, rows_own), 1)
    count_col = jnp.sum(
        jnp.where(diag, counts[...].astype(F32), 0.0), -1, keepdims=True
    )
    own_scale = t_rstd / count_col

    finish(row_recv.at[pl.ds(0, zs - 1)], 3)
    concept = jnp.sum(row_recv[...].astype(F32), 0)
    c_mean = jnp.sum(jnp.sum(concept, -1, keepdims=True), 0, keepdims=True) / width
    c_diff = concept - c_mean
    c_var = jnp.sum(jnp.sum(c_diff * c_diff, -1, keepdims=True), 0, keepdims=True) / width
    c32[...] = c_diff * lax.rsqrt(c_var + EPSILON)
    for c in range(width // LANES):
        c_row[:, c * LANES : (c + 1) * LANES] = c32[c : c + 1, :]
    at_pos = iota((tok_len, 1), 0) == own_pos
    normed = jnp.where(at_pos, c_row[...], tok_hat).astype(BF)
    lab_lane = iota((tok_len, LANES), 1)
    lab_row = iota((tok_len, LANES), 0)
    id_high = lax.div(own_id, 64)
    id_low = lax.rem(own_id, 64)
    label = jnp.where(lab_lane == 0, own_time, 0)
    label = jnp.where((lab_lane == 1) & (lab_row == own_pos), 1, label)
    label = jnp.where(lab_lane == 2, id_high, label)
    label = jnp.where(lab_lane == 3, id_low, label)
    label = label.astype(F32).astype(BF)
    for c in range(groups):
        tok_msg[c, :, :group_w] = normed[:, c * group_w : (c + 1) * group_w]
        tok_msg[c, :, group_w:] = label
    tok_recv[f] = tok_msg[grp]

    def send_tok(j, c):
        peer = lax.rem(f + j, ns)
        remote(tok_msg.at[lax.div(peer, m)], tok_recv.at[f], 4, (z, peer)).start()
        return c

    lax.fori_loop(1, ns, send_tok, 0)
    finish(w_recv.at[pl.ds(0, (m - 1) * slice_w)], 1)
    finish(tok_recv.at[pl.ds(0, ns - 1)], 4)

    all_rows = tok_recv[...].astype(F32).reshape(ns * tok_len, group_w + LANES)
    toks = all_rows[:, :group_w]
    labels = all_rows[:, group_w:]
    times = labels[:, 0:1].astype(jnp.int32)
    placed = labels[:, 1:2]
    pick_time = (iota((ns * tok_len, buckets), 1) == times).astype(F32).astype(BF)
    shift = jnp.dot(pick_time, mod_all[:buckets, :], preferred_element_type=F32)
    scale = 1.0 + jnp.dot(pick_time, mod_all[buckets:, :], preferred_element_type=F32)
    modulated = (scale * toks + shift).astype(BF)
    terms = jnp.dot(modulated, w_recv[...], preferred_element_type=F32)
    part[...] = terms.reshape(ns, tok_len, block)
    concepts = jnp.sum((toks * placed).reshape(ns, tok_len, group_w), 1)
    scales = jnp.sum((scale * placed).reshape(ns, tok_len, group_w), 1)
    a_high, a_low = split_two(scales)
    b_high, b_low = split_two(scales * concepts)
    extra = jnp.dot(
        jnp.concatenate([a_high, a_low, b_high, b_low], 0),
        w_recv[...],
        preferred_element_type=F32,
    )
    side[:, 0, :] = extra[:ns] + extra[ns : 2 * ns]
    side[:, 1, :] = extra[2 * ns : 3 * ns] + extra[3 * ns :]
    part_recv[f] = part[f]
    side_recv[f] = side[f]

    def send_part(j, c):
        peer = lax.rem(f + j, ns)
        remote(part.at[peer], part_recv.at[f], 5, (z, peer)).start()
        remote(side.at[peer], side_recv.at[f], 6, (z, peer)).start()
        return c

    lax.fori_loop(1, ns, send_part, 0)

    labels_s = labels.reshape(ns, tok_len, LANES)[:, 0, :]
    pick_s = (
        (iota((ns, buckets), 1) == labels_s[:, 0:1].astype(jnp.int32)).astype(F32).astype(BF)
    )
    scale_own = 1.0 + jnp.dot(pick_s, modp[buckets:, :], preferred_element_type=F32)
    own_row = iota((group_w, LANES), 0)
    own_col = iota((group_w, LANES), 1)
    own_place = ((own_row == own_col + r * slice_w) & (own_col < slice_w)).astype(F32).astype(BF)
    concept_own = jnp.dot(concepts.astype(BF), own_place, preferred_element_type=F32)

    finish(part_recv.at[pl.ds(0, ns - 1)], 5)
    finish(side_recv.at[pl.ds(0, ns - 1)], 6)
    per = block // LANES
    for c in range(m):
        total = part_recv[c]
        extras = side_recv[c]
        for a in range(1, groups):
            total += part_recv[a * m + c]
            extras += side_recv[a * m + c]
        kv[:, c * block : (c + 1) * block] = total
        for b in range(per):
            s1_32[c * per + b : c * per + b + 1, :] = extras[0:1, b * LANES : (b + 1) * LANES]
            s2_32[c * per + b : c * per + b + 1, :] = extras[1:2, b * LANES : (b + 1) * LANES]

    kv_all = kv[...] + bias[...]
    pos_f = at_pos.astype(F32)
    gains = gain[...]
    raw_row = jnp.sum(kv_all[:, :head_w] * pos_f, 0, keepdims=True)
    key_parts = []
    for h in range(heads):
        raw = kv_all[:, h * LANES : (h + 1) * LANES]
        inv = lax.rsqrt(jnp.mean(raw * raw, -1, keepdims=True) + EPSILON)
        key_parts.append((raw * inv * gains).astype(BF).astype(F32))
        raw32[h : h + 1, :] = raw_row[:, h * LANES : (h + 1) * LANES]
    key_txt = jnp.concatenate(key_parts, 1)
    val_txt = kv_all[:, head_w:].astype(BF).astype(F32)
    own_head = iota((heads * tok_len, head_w), 0) // tok_len == iota(
        (heads * tok_len, head_w), 1
    ) // LANES
    key_diag = jnp.where(own_head, jnp.concatenate([key_txt] * heads, 0), 0.0).astype(BF)
    val_diag = jnp.where(own_head, jnp.concatenate([val_txt] * heads, 0), 0.0).astype(BF)
    s_txt = (
        lax.dot_general(key_diag, q[...], NT_DIMS, preferred_element_type=F32) * inv_root
    ).reshape(heads, tok_len, n_img)
    g_txt = lax.dot_general(val_diag, g[...], NT_DIMS, preferred_element_type=F32).reshape(
        heads, tok_len, n_img
    )
    top_img = m_img[...]
    top = jnp.maximum(top_img, jnp.max(s_txt, 1, keepdims=True))
    raised = jnp.exp(s_txt - top)
    alpha = jnp.exp(top_img - top)
    denom = alpha * l_img[...] + jnp.sum(raised, 1, keepdims=True)
    probs = raised / denom
    delta = alpha * d_img[...] / denom + jnp.sum(
        probs.astype(BF).astype(F32) * g_txt, 1, keepdims=True
    )
    pos_3 = (iota((1, tok_len, 1), 1) == own_pos).astype(F32)
    p_pos = jnp.sum(probs * pos_3, 1)
    g_pos = jnp.sum(g_txt * pos_3, 1)
    d_score = p_pos * (g_pos - delta[:, 0, :]) * inv_root
    p_high, p_low = split_two(p_pos)
    d_high, d_low = split_two(d_score)
    d_val = jnp.dot(
        jnp.concatenate([p_high.astype(F32), p_low.astype(F32)], 0).astype(BF),
        g[...],
        preferred_element_type=F32,
    )
    d_key = jnp.dot(
        jnp.concatenate([d_high.astype(F32), d_low.astype(F32)], 0).astype(BF),
        q[...],
        preferred_element_type=F32,
    )
    d_val = d_val[:heads] + d_val[heads:]
    d_key = d_key[:heads] + d_key[heads:]
    dkv32[...] = jnp.zeros(dkv32.shape, F32)
    for h in range(heads):
        dkv32[h : h + 1, :] = d_key[h : h + 1, h * LANES : (h + 1) * LANES]
        dkv32[heads + h : heads + h + 1, :] = d_val[h : h + 1, h * LANES : (h + 1) * LANES]
    raw_pos = raw32[...]
    inv_pos = lax.rsqrt(jnp.mean(raw_pos * raw_pos, -1, keepdims=True) + EPSILON)
    n_pos = raw_pos * inv_pos
    d_norm = dkv32[:heads, :] * gains
    dkv32[:heads, :] = inv_pos * (d_norm - n_pos * jnp.mean(d_norm * n_pos, -1, keepdims=True))
    dkv_rows = dkv32[: 2 * heads, :].astype(BF).astype(F32)
    mean_1 = jnp.sum(jnp.sum(dkv_rows * s1_32[...], -1, keepdims=True), 0, keepdims=True) / width
    mean_2 = jnp.sum(jnp.sum(dkv_rows * s2_32[...], -1, keepdims=True), 0, keepdims=True) / width
    for c, value in enumerate((mean_1, mean_2)):
        high, low = split_two(value)
        at = 2 * heads + 2 * c
        dkv32[at : at + 1, :] = jnp.broadcast_to(high.astype(F32), (1, LANES))
        dkv32[at + 1 : at + 2, :] = jnp.broadcast_to(low.astype(F32), (1, LANES))
    dkv_own[...] = dkv32[...].astype(BF)
    dkv_recv[f] = dkv_own[...]

    def send_dkv(j, c):
        remote(dkv_own, dkv_recv.at[f], 7, (z, lax.rem(f + j, ns))).start()
        return c

    lax.fori_loop(1, ns, send_dkv, 0)
    finish(dkv_recv.at[pl.ds(0, ns - 1)], 7)
    dkv_wide[...] = dkv_recv[...].astype(F32)
    grads = jnp.zeros((ns, slice_w), F32)
    for c in range(2 * heads):
        grads += lax.dot_general(
            dkv_wide[:, c, :].astype(BF),
            weight[:, c * LANES : (c + 1) * LANES],
            NT_DIMS,
            preferred_element_type=F32,
        )
    at = 2 * heads
    mean_1 = (dkv_wide[:, at, :] + dkv_wide[:, at + 1, :])[:, :slice_w]
    mean_2 = (dkv_wide[:, at + 2, :] + dkv_wide[:, at + 3, :])[:, :slice_w]
    row_grad = grads * scale_own[:, :slice_w] - mean_1 - concept_own[:, :slice_w] * mean_2
    g_own[:, :slice_w] = row_grad.astype(BF)
    g_own[:, slice_w:] = labels_s[:, : LANES - slice_w].astype(BF)
    g_recv[z] = g_own[...]

    def send_grad(j, c):
        remote(g_own, g_recv.at[z], 8, (lax.rem(z + j, zs), f)).start()
        return c

    lax.fori_loop(1, zs, send_grad, 0)
    finish(g_recv.at[pl.ds(0, zs - 1)], 8)
    every = g_recv[...].astype(F32).reshape(zs * ns, LANES)
    who = (every[:, slice_w + 2 : slice_w + 3] * 64.0 + every[:, slice_w + 3 : slice_w + 4]).astype(
        jnp.int32
    )
    belongs = (iota((zs * ns, rows_own), 1) + z * rows_own == who).astype(F32).astype(BF)
    summed = lax.dot_general(
        belongs, every.astype(BF), TN_DIMS, preferred_element_type=F32
    )
    out[...] = (summed * own_scale)[:, :slice_w]

    drain(id_buf.at[pl.ds(0, zs - 1)], 0)
    drain(w_recv.at[pl.ds(0, (m - 1) * slice_w)], 1)
    drain(mod_recv.at[pl.ds(0, m - 1)], 2)
    drain(row_recv.at[pl.ds(0, zs - 1)], 3)
    drain(tok_recv.at[pl.ds(0, ns - 1)], 4)
    drain(part_recv.at[pl.ds(0, ns - 1)], 5)
    drain(side_recv.at[pl.ds(0, ns - 1)], 6)
    drain(dkv_recv.at[pl.ds(0, ns - 1)], 7)
    drain(g_recv.at[pl.ds(0, zs - 1)], 8)


def shards(
    txt_tokens,
    concept_table,
    concept_ids,
    positions,
    timesteps,
    counts,
    mod_table,
    kv_weight,
    kv_bias,
    key_gain,
    img_query,
    img_key,
    img_value,
    out_grad,
):
    ns = lax.axis_size("fsdp")
    zs = lax.axis_size("dp")
    m = 8 if ns % 16 == 0 else 4
    tok_len, width = txt_tokens.shape[1:]
    slice_w, kv_w = kv_weight.shape
    head_w = kv_w // 2
    heads = head_w // LANES
    n_img = img_query.shape[1]
    buckets = mod_table.shape[0]
    rows_own = concept_table.shape[0]
    block = kv_w // m
    group_w = slice_w * m
    n_c = width // LANES
    slot = (2 * heads + 4 + 15) // 16 * 16

    modp = jnp.pad(
        mod_table.transpose(1, 0, 2).reshape(2 * buckets, slice_w), ((0, 0), (0, LANES - slice_w))
    )
    vm = pl.BlockSpec(memory_space=pltpu.VMEM)
    sm = pl.BlockSpec(memory_space=pltpu.SMEM)
    hb = pl.BlockSpec(memory_space=pl.ANY)
    image = pltpu.VMEM((n_img, head_w), BF)
    stat = pltpu.VMEM((heads, 1, n_img), F32)
    return pl.pallas_call(
        functools.partial(step_kernel, (zs, ns, m)),
        out_shape=jax.ShapeDtypeStruct((rows_own, slice_w), F32),
        in_specs=[sm] * 3 + [vm] * 7 + [hb] * 4,
        out_specs=vm,
        scratch_shapes=[
            image,
            image,
            image,
            image,
            pltpu.VMEM((zs, 1, LANES), jnp.int32),
            pltpu.VMEM((1, LANES), jnp.int32),
            pltpu.VMEM((zs, n_c, LANES), F32),
            pltpu.VMEM((zs, n_c, LANES), BF),
            pltpu.VMEM((zs, n_c, LANES), BF),
            pltpu.VMEM((n_c, LANES), F32),
            pltpu.VMEM((1, width), F32),
            pltpu.VMEM((ns // m, tok_len, group_w + LANES), BF),
            pltpu.VMEM((ns, tok_len, group_w + LANES), BF),
            pltpu.VMEM((group_w, block), BF),
            pltpu.VMEM((m, 2 * buckets, LANES), BF),
            pltpu.VMEM((2 * buckets, group_w), BF),
            pltpu.VMEM((ns, tok_len, block), F32),
            pltpu.VMEM((ns, tok_len, block), F32),
            pltpu.VMEM((ns, 2, block), F32),
            pltpu.VMEM((ns, 2, block), F32),
            pltpu.VMEM((tok_len, kv_w), F32),
            stat,
            stat,
            stat,
            pltpu.VMEM((slot, LANES), F32),
            pltpu.VMEM((heads, LANES), F32),
            pltpu.VMEM((2 * heads, LANES), F32),
            pltpu.VMEM((2 * heads, LANES), F32),
            pltpu.VMEM((slot, LANES), BF),
            pltpu.VMEM((ns, slot, LANES), BF),
            pltpu.VMEM((ns, slot, LANES), F32),
            pltpu.VMEM((ns, LANES), BF),
            pltpu.VMEM((zs, ns, LANES), BF),
            pltpu.SemaphoreType.DMA((4,)),
            pltpu.SemaphoreType.DMA((9,)),
            pltpu.SemaphoreType.DMA((9,)),
        ],
        compiler_params=pltpu.CompilerParams(collective_id=0, has_side_effects=True),
    )(
        concept_ids,
        positions,
        timesteps,
        txt_tokens[0],
        concept_table,
        counts[None, :],
        modp,
        kv_weight,
        kv_bias[None, :],
        key_gain[None, :],
        img_query[0],
        img_key[0],
        img_value[0],
        out_grad[0],
    )


def solution(mesh):
    placed = (
        P(("dp", "fsdp"), None, None),
        P("dp", None),
        P(("dp", "fsdp")),
        P(("dp", "fsdp")),
        P(("dp", "fsdp")),
        P("dp"),
        P(None, None, "fsdp"),
        P("fsdp", None),
        P(),
        P(),
        P(("dp", "fsdp"), None, None),
        P(("dp", "fsdp"), None, None),
        P(("dp", "fsdp"), None, None),
        P(("dp", "fsdp"), None, None),
    )
    return jax.shard_map(
        shards, mesh=mesh, in_specs=placed, out_specs=P("dp", "fsdp"), check_vma=False
    )
```

```python
import functools
import jax
import jax.numpy as jnp
from jax import lax
from jax.experimental import pallas as pl
from jax.experimental.pallas import tpu as pltpu
from jax.sharding import PartitionSpec as P

EPSILON = 1e-06
LANES = 128
BF = jnp.bfloat16
F32 = jnp.float32
MESH = pl.DeviceIdType.MESH
NT_DIMS = (((1,), (1,)), ((), ()))
TN_DIMS = (((0,), (0,)), ((), ()))


def split_two(values):
    high = values.astype(BF)
    low = (values - high.astype(F32)).astype(BF)
    return high, low


def iota(shape, axis):
    return lax.broadcasted_iota(jnp.int32, shape, axis)


def far_first(sizes):
    steps = [(a, b, c) for a in range(sizes[0]) for b in range(sizes[1]) for c in range(2)]

    def hops(step):
        return sum(min(d, n - d) for d, n in zip(step[:2], sizes))

    return sorted(steps[1:], key=lambda step: (-hops(step), step))


def step_kernel(
    dims,
    ids_s,
    pos_s,
    time_s,
    tok,
    counts,
    mods,
    bias,
    gain,
    table_any,
    weight_any,
    q_any,
    k_any,
    v_any,
    g_any,
    out,
    table,
    weight,
    q,
    k,
    v,
    g,
    mod32,
    modp,
    id_buf,
    id_own,
    row32,
    row_send,
    row_recv,
    c32,
    c_row,
    tok_msg,
    tok_recv,
    c_msg,
    c_recv,
    w_recv,
    mod_recv,
    mod_all,
    part,
    part_recv,
    late,
    late_recv,
    kv,
    m_img,
    l_img,
    d_img,
    dkv32,
    raw32,
    s1_32,
    s2_32,
    dkv_own,
    dkv_recv,
    dkv_wide,
    g_own,
    g_recv,
    load_sem,
    send_sem,
    recv_sem,
):
    zs, nx, ny = dims
    ns = nx * ny * 2
    m = ny * 2
    z = lax.axis_index("dp")
    f = lax.axis_index("fsdp")
    groups = nx
    r = lax.rem(f, m)
    grp = lax.div(f, m)
    tok_len, width = tok.shape
    slice_w = weight.shape[0]
    kv_w = weight.shape[1]
    head_w = kv_w // 2
    heads = head_w // LANES
    block = kv_w // m
    group_w = slice_w * m
    n_img = q.shape[0]
    rows_own = table.shape[0]
    buckets = mods.shape[0]
    inv_root = 1.0 / (LANES**0.5)

    my_y = lax.div(r, 2)
    my_c = lax.rem(r, 2)
    x_at = [lax.rem(grp + d, nx) for d in range(nx)]
    y_at = [lax.rem(my_y + d, ny) * 2 for d in range(ny)]
    c_at = [my_c, 1 - my_c]
    plane = [(x_at[a], y_at[b] + c_at[c]) for a, b, c in far_first((nx, ny))]
    mates = [y_at[b] + c_at[c] for a, b, c in far_first((nx, ny)) if a == 0]
    line = [
        lax.rem(z + d, zs) for d in sorted(range(1, zs), key=lambda d: (-min(d, zs - d), d))
    ]

    table_load = pltpu.make_async_copy(table_any, table, load_sem.at[0])
    weight_load = pltpu.make_async_copy(weight_any, weight, load_sem.at[1])
    loads = [
        pltpu.make_async_copy(src, dst, load_sem.at[2 + i])
        for i, (src, dst) in enumerate(((q_any, q), (k_any, k), (v_any, v), (g_any, g)))
    ]
    weight_load.start()
    table_load.start()
    for copy in loads:
        copy.start()

    barrier = pltpu.get_barrier_semaphore()
    for peer in line:
        pl.semaphore_signal(barrier, inc=1, device_id=(peer, f), device_id_type=MESH)
    for gx, inner in plane:
        pl.semaphore_signal(
            barrier, inc=1, device_id=(z, gx * m + inner), device_id_type=MESH
        )

    own_id = ids_s[0]
    own_pos = pos_s[0]
    own_time = time_s[0]
    id_own[...] = jnp.full(id_own.shape, own_id, jnp.int32)
    id_buf[z] = id_own[...]

    tok_f = tok[...].astype(F32)
    centre = jnp.mean(tok_f, -1, keepdims=True)
    spread = jnp.mean((tok_f - centre) ** 2, -1, keepdims=True)
    tok_hat = ((tok_f - centre) * lax.rsqrt(spread + EPSILON)).astype(BF)
    at_pos = iota((tok_len, 1), 0) == own_pos
    lab_lane = iota((tok_len, LANES), 1)
    lab_row = iota((tok_len, LANES), 0)
    id_high = lax.div(own_id, 64)
    id_low = lax.rem(own_id, 64)
    label = jnp.where(lab_lane == 0, own_time, 0)
    label = jnp.where((lab_lane == 1) & (lab_row == own_pos), 1, label)
    label = jnp.where(lab_lane == 2, id_high, label)
    label = jnp.where(lab_lane == 3, id_low, label)
    label = label.astype(F32).astype(BF)
    for c in range(groups):
        tok_msg[c, :, :group_w] = tok_hat[:, c * group_w : (c + 1) * group_w]
        tok_msg[c, :, group_w:] = label
    tok_recv[f] = tok_msg[grp]

    mod32[...] = jnp.zeros(mod32.shape, F32)
    mod32[:, :, :slice_w] = mods[...].astype(F32)
    modp[:buckets, :] = mod32[:, 0, :].astype(BF)
    modp[buckets:, :] = mod32[:, 1, :].astype(BF)
    mod_recv[r] = modp[...]
    weight_load.wait()
    w_recv[pl.ds(pl.multiple_of(r * slice_w, 16), slice_w), :] = weight[
        :, pl.ds(pl.multiple_of(r * block, LANES), block)
    ]

    pl.semaphore_wait(barrier, zs - 1 + ns - 1)

    def remote(src, dst, phase, device):
        return pltpu.make_async_remote_copy(
            src_ref=src,
            dst_ref=dst,
            send_sem=send_sem.at[phase],
            recv_sem=recv_sem.at[phase],
            device_id=device,
            device_id_type=MESH,
        )

    def finish(ref, phase):
        pltpu.make_async_copy(ref, ref, recv_sem.at[phase]).wait()

    def drain(ref, phase):
        pltpu.make_async_copy(ref, ref, send_sem.at[phase]).wait()

    for peer in line:
        remote(id_own, id_buf.at[z], 0, (peer, f)).start()

    for peer in mates:
        remote(modp, mod_recv.at[r], 2, (z, grp * m + peer)).start()
    for peer in mates:
        remote(
            weight.at[:, pl.ds(pl.multiple_of(peer * block, LANES), block)],
            w_recv.at[pl.ds(pl.multiple_of(r * slice_w, 16), slice_w), :],
            1,
            (z, grp * m + peer),
        ).start()

    for gx, inner in plane:
        remote(tok_msg.at[gx], tok_recv.at[f], 4, (z, gx * m + inner)).start()

    for copy in loads:
        copy.wait()

    def image_head(h, c):
        lanes = pl.ds(pl.multiple_of(h * LANES, LANES), LANES)
        scores = (
            lax.dot_general(k[:, lanes], q[:, lanes], NT_DIMS, preferred_element_type=F32)
            * inv_root
        )
        grads = lax.dot_general(v[:, lanes], g[:, lanes], NT_DIMS, preferred_element_type=F32)
        top = jnp.max(scores, 0, keepdims=True)
        raised = jnp.exp(scores - top)
        m_img[h] = top
        l_img[h] = jnp.sum(raised, 0, keepdims=True)
        d_img[h] = jnp.sum(raised.astype(BF).astype(F32) * grads, 0, keepdims=True)
        return c

    half = heads // 2
    lax.fori_loop(0, half, image_head, 0)
    table_load.wait()

    finish(id_buf.at[pl.ds(0, zs - 1)], 0)
    wanted = id_buf[:, 0, :][:, :1]
    pick = (iota((zs, rows_own), 1) + z * rows_own == wanted).astype(F32).astype(BF)
    rows = jnp.dot(pick, table[...], preferred_element_type=F32)
    for c in range(width // LANES):
        row32[:, c, :] = rows[:, c * LANES : (c + 1) * LANES]
    row_send[...] = row32[...].astype(BF)
    row_recv[z] = row_send[z]
    for peer in line:
        remote(row_send.at[peer], row_recv.at[z], 3, (peer, f)).start()

    lax.fori_loop(half, heads, image_head, 0)

    finish(mod_recv.at[pl.ds(0, m - 1)], 2)
    lane_row = iota((LANES, group_w), 0)
    lane_col = iota((LANES, group_w), 1)
    mod_sum = jnp.zeros((2 * buckets, group_w), F32)
    for c in range(m):
        place = ((lane_col == lane_row + c * slice_w) & (lane_row < slice_w)).astype(F32)
        mod_sum += jnp.dot(mod_recv[c], place.astype(BF), preferred_element_type=F32)
    mod_all[...] = mod_sum.astype(BF)

    table_f = table[...].astype(F32)
    t_centre = jnp.mean(table_f, -1, keepdims=True)
    t_spread = jnp.mean((table_f - t_centre) ** 2, -1, keepdims=True)
    t_rstd = lax.rsqrt(t_spread + EPSILON)
    diag = iota((rows_own, rows_own), 0) == iota((rows_own, rows_own), 1)
    own_scale = jnp.sum(jnp.where(diag, t_rstd, 0.0), 0, keepdims=True) / counts[...].astype(F32)

    finish(tok_recv.at[pl.ds(0, ns - 1)], 4)
    all_rows = tok_recv[...].astype(F32).reshape(ns * tok_len, group_w + LANES)
    toks = all_rows[:, :group_w]
    labels = all_rows[:, group_w:]
    times = labels[:, 0:1].astype(jnp.int32)
    pick_time = (iota((ns * tok_len, buckets), 1) == times).astype(F32).astype(BF)
    shift = jnp.dot(pick_time, mod_all[:buckets, :], preferred_element_type=F32)
    scale = 1.0 + jnp.dot(pick_time, mod_all[buckets:, :], preferred_element_type=F32)
    modulated = (scale * toks + shift).astype(BF)
    shift_s = shift.reshape(ns, tok_len, group_w)[:, 0, :]
    scale_s = scale.reshape(ns, tok_len, group_w)[:, 0, :]
    a_high, a_low = split_two(scale_s)
    finish(w_recv.at[pl.ds(0, (m - 1) * slice_w)], 1)
    terms = jnp.dot(modulated, w_recv[...], preferred_element_type=F32)
    extra = jnp.dot(
        jnp.concatenate([a_high, a_low], 0), w_recv[...], preferred_element_type=F32
    )
    sums = (extra[:ns] + extra[ns:]).reshape(ns, 1, block)
    placed = labels.reshape(ns, tok_len, LANES)[:, :, 1:2]
    part[...] = jnp.where(placed > 0.5, sums, terms.reshape(ns, tok_len, block))
    part_recv[f] = part[f]
    for gx, inner in plane:
        peer = gx * m + inner
        remote(part.at[peer], part_recv.at[f], 5, (z, peer)).start()

    finish(row_recv.at[pl.ds(0, zs - 1)], 3)
    concept = jnp.sum(row_recv[...].astype(F32), 0)
    c_mean = jnp.sum(jnp.sum(concept, -1, keepdims=True), 0, keepdims=True) / width
    c_diff = concept - c_mean
    c_var = jnp.sum(jnp.sum(c_diff * c_diff, -1, keepdims=True), 0, keepdims=True) / width
    c32[...] = (c_diff * lax.rsqrt(c_var + EPSILON)).astype(BF).astype(F32)
    for c in range(width // LANES):
        c_row[:, c * LANES : (c + 1) * LANES] = c32[c : c + 1, :]
    for c in range(groups):
        c_msg[c] = c_row[:, c * group_w : (c + 1) * group_w]
    c_recv[f] = c_msg[grp]
    for gx, inner in plane:
        remote(c_msg.at[gx], c_recv.at[f], 9, (z, gx * m + inner)).start()

    labels_s = labels.reshape(ns, tok_len, LANES)[:, 0, :]
    pick_s = (
        (iota((ns, buckets), 1) == labels_s[:, 0:1].astype(jnp.int32)).astype(F32).astype(BF)
    )
    scale_own = 1.0 + jnp.dot(pick_s, modp[buckets:, :], preferred_element_type=F32)
    own_row = iota((group_w, LANES), 0)
    own_col = iota((group_w, LANES), 1)
    own_place = ((own_row == own_col + r * slice_w) & (own_col < slice_w)).astype(F32).astype(BF)

    finish(c_recv.at[pl.ds(0, ns - 1)], 9)
    concepts = c_recv[:, 0, :]
    scaled = scale_s * concepts
    b_high, b_low = split_two(scaled)
    extra = jnp.dot(
        jnp.concatenate([(scaled + shift_s).astype(BF), b_high, b_low], 0),
        w_recv[...],
        preferred_element_type=F32,
    )
    late[:, 0, :] = extra[:ns]
    late[:, 1, :] = extra[ns : 2 * ns] + extra[2 * ns :]
    late_recv[f] = late[f]
    for gx, inner in plane:
        peer = gx * m + inner
        remote(late.at[peer], late_recv.at[f], 6, (z, peer)).start()
    concept_own = jnp.dot(concepts.astype(BF), own_place, preferred_element_type=F32)

    finish(part_recv.at[pl.ds(0, ns - 1)], 5)
    finish(late_recv.at[pl.ds(0, ns - 1)], 6)
    per = block // LANES
    pos_f = at_pos.astype(F32)
    for c in range(m):
        total = part_recv[c]
        extras = late_recv[c]
        for a in range(1, groups):
            total += part_recv[a * m + c]
            extras += late_recv[a * m + c]
        first = jnp.sum(total * pos_f, 0, keepdims=True)
        kv[:, c * block : (c + 1) * block] = jnp.where(at_pos, extras[0:1, :], total)
        for b in range(per):
            s1_32[c * per + b : c * per + b + 1, :] = first[:, b * LANES : (b + 1) * LANES]
            s2_32[c * per + b : c * per + b + 1, :] = extras[1:2, b * LANES : (b + 1) * LANES]

    kv_all = kv[...] + bias[...]
    gains = gain[...]
    raw_row = jnp.sum(kv_all[:, :head_w] * pos_f, 0, keepdims=True)
    key_parts = []
    for h in range(heads):
        raw = kv_all[:, h * LANES : (h + 1) * LANES]
        inv = lax.rsqrt(jnp.mean(raw * raw, -1, keepdims=True) + EPSILON)
        key_parts.append((raw * inv * gains).astype(BF).astype(F32))
        raw32[h : h + 1, :] = raw_row[:, h * LANES : (h + 1) * LANES]
    key_txt = jnp.concatenate(key_parts, 1)
    val_txt = kv_all[:, head_w:].astype(BF).astype(F32)
    own_head = iota((heads * tok_len, head_w), 0) // tok_len == iota(
        (heads * tok_len, head_w), 1
    ) // LANES
    key_diag = jnp.where(own_head, jnp.concatenate([key_txt] * heads, 0), 0.0).astype(BF)
    val_diag = jnp.where(own_head, jnp.concatenate([val_txt] * heads, 0), 0.0).astype(BF)
    s_txt = (
        lax.dot_general(key_diag, q[...], NT_DIMS, preferred_element_type=F32) * inv_root
    ).reshape(heads, tok_len, n_img)
    g_txt = lax.dot_general(val_diag, g[...], NT_DIMS, preferred_element_type=F32).reshape(
        heads, tok_len, n_img
    )
    top_img = m_img[...]
    top = jnp.maximum(top_img, jnp.max(s_txt, 1, keepdims=True))
    raised = jnp.exp(s_txt - top)
    alpha = jnp.exp(top_img - top)
    denom = alpha * l_img[...] + jnp.sum(raised, 1, keepdims=True)
    probs = raised / denom
    delta = alpha * d_img[...] / denom + jnp.sum(
        probs.astype(BF).astype(F32) * g_txt, 1, keepdims=True
    )
    pos_3 = (iota((1, tok_len, 1), 1) == own_pos).astype(F32)
    p_pos = jnp.sum(probs * pos_3, 1)
    g_pos = jnp.sum(g_txt * pos_3, 1)
    d_score = p_pos * (g_pos - delta[:, 0, :]) * inv_root
    p_high, p_low = split_two(p_pos)
    d_high, d_low = split_two(d_score)
    d_val = jnp.dot(
        jnp.concatenate([p_high.astype(F32), p_low.astype(F32)], 0).astype(BF),
        g[...],
        preferred_element_type=F32,
    )
    d_key = jnp.dot(
        jnp.concatenate([d_high.astype(F32), d_low.astype(F32)], 0).astype(BF),
        q[...],
        preferred_element_type=F32,
    )
    d_val = d_val[:heads] + d_val[heads:]
    d_key = d_key[:heads] + d_key[heads:]
    dkv32[...] = jnp.zeros(dkv32.shape, F32)
    for h in range(heads):
        dkv32[h : h + 1, :] = d_key[h : h + 1, h * LANES : (h + 1) * LANES]
        dkv32[heads + h : heads + h + 1, :] = d_val[h : h + 1, h * LANES : (h + 1) * LANES]
    raw_pos = raw32[...]
    inv_pos = lax.rsqrt(jnp.mean(raw_pos * raw_pos, -1, keepdims=True) + EPSILON)
    n_pos = raw_pos * inv_pos
    d_norm = dkv32[:heads, :] * gains
    dkv32[:heads, :] = inv_pos * (d_norm - n_pos * jnp.mean(d_norm * n_pos, -1, keepdims=True))
    dkv_rows = dkv32[: 2 * heads, :].astype(BF).astype(F32)
    mean_1 = jnp.sum(jnp.sum(dkv_rows * s1_32[...], -1, keepdims=True), 0, keepdims=True) / width
    mean_2 = jnp.sum(jnp.sum(dkv_rows * s2_32[...], -1, keepdims=True), 0, keepdims=True) / width
    for c, value in enumerate((mean_1, mean_2)):
        high, low = split_two(value)
        at = 2 * heads + 2 * c
        dkv32[at : at + 1, :] = jnp.broadcast_to(high.astype(F32), (1, LANES))
        dkv32[at + 1 : at + 2, :] = jnp.broadcast_to(low.astype(F32), (1, LANES))
    dkv_own[...] = dkv32[...].astype(BF)
    dkv_recv[f] = dkv_own[...]

    for gx, inner in plane:
        remote(dkv_own, dkv_recv.at[f], 7, (z, gx * m + inner)).start()
    finish(dkv_recv.at[pl.ds(0, ns - 1)], 7)
    dkv_wide[...] = dkv_recv[...].astype(F32)
    grads = jnp.zeros((ns, slice_w), F32)
    for c in range(2 * heads):
        grads += lax.dot_general(
            dkv_wide[:, c, :].astype(BF),
            weight[:, c * LANES : (c + 1) * LANES],
            NT_DIMS,
            preferred_element_type=F32,
        )
    at = 2 * heads
    mean_1 = (dkv_wide[:, at, :] + dkv_wide[:, at + 1, :])[:, :slice_w]
    mean_2 = (dkv_wide[:, at + 2, :] + dkv_wide[:, at + 3, :])[:, :slice_w]
    row_grad = grads * scale_own[:, :slice_w] - mean_1 - concept_own[:, :slice_w] * mean_2
    g_own[:, :slice_w] = row_grad.astype(BF)
    g_own[:, slice_w:] = labels_s[:, : LANES - slice_w].astype(BF)
    g_recv[z] = g_own[...]

    for peer in line:
        remote(g_own, g_recv.at[z], 8, (peer, f)).start()
    finish(g_recv.at[pl.ds(0, zs - 1)], 8)
    every = g_recv[...].astype(F32).reshape(zs * ns, LANES)
    who = (every[:, slice_w + 2 : slice_w + 3] * 64.0 + every[:, slice_w + 3 : slice_w + 4]).astype(
        jnp.int32
    )
    belongs = (iota((zs * ns, rows_own), 1) + z * rows_own == who).astype(F32).astype(BF)
    summed = lax.dot_general(
        every.astype(BF), belongs, TN_DIMS, preferred_element_type=F32
    )
    out[...] = summed[:slice_w, :] * own_scale

    drain(id_buf.at[pl.ds(0, zs - 1)], 0)
    drain(w_recv.at[pl.ds(0, (m - 1) * slice_w)], 1)
    drain(mod_recv.at[pl.ds(0, m - 1)], 2)
    drain(row_recv.at[pl.ds(0, zs - 1)], 3)
    drain(tok_recv.at[pl.ds(0, ns - 1)], 4)
    drain(part_recv.at[pl.ds(0, ns - 1)], 5)
    drain(late_recv.at[pl.ds(0, ns - 1)], 6)
    drain(dkv_recv.at[pl.ds(0, ns - 1)], 7)
    drain(g_recv.at[pl.ds(0, zs - 1)], 8)
    drain(c_recv.at[pl.ds(0, ns - 1)], 9)


def shards(
    txt_tokens,
    concept_table,
    concept_ids,
    positions,
    timesteps,
    counts,
    mod_table,
    kv_weight,
    kv_bias,
    key_gain,
    img_query,
    img_key,
    img_value,
    out_grad,
):
    ns = lax.axis_size("fsdp")
    zs = lax.axis_size("dp")
    nx, ny = (4, 4) if ns == 32 else (2, 2)
    m = ny * 2
    tok_len, width = txt_tokens.shape[1:]
    slice_w, kv_w = kv_weight.shape
    head_w = kv_w // 2
    heads = head_w // LANES
    n_img = img_query.shape[1]
    buckets = mod_table.shape[0]
    rows_own = concept_table.shape[0]
    block = kv_w // m
    group_w = slice_w * m
    n_c = width // LANES
    slot = (2 * heads + 4 + 15) // 16 * 16

    vm = pl.BlockSpec(memory_space=pltpu.VMEM)
    sm = pl.BlockSpec(memory_space=pltpu.SMEM)
    hb = pl.BlockSpec(memory_space=pl.ANY)
    image = pltpu.VMEM((n_img, head_w), BF)
    stat = pltpu.VMEM((heads, 1, n_img), F32)
    grad_t = pl.pallas_call(
        functools.partial(step_kernel, (zs, nx, ny)),
        out_shape=jax.ShapeDtypeStruct((slice_w, rows_own), F32),
        in_specs=[sm] * 3 + [vm] * 5 + [hb] * 6,
        out_specs=vm,
        scratch_shapes=[
            pltpu.VMEM((rows_own, width), BF),
            pltpu.VMEM((slice_w, kv_w), BF),
            image,
            image,
            image,
            image,
            pltpu.VMEM((buckets, 2, LANES), F32),
            pltpu.VMEM((2 * buckets, LANES), BF),
            pltpu.VMEM((zs, 1, LANES), jnp.int32),
            pltpu.VMEM((1, LANES), jnp.int32),
            pltpu.VMEM((zs, n_c, LANES), F32),
            pltpu.VMEM((zs, n_c, LANES), BF),
            pltpu.VMEM((zs, n_c, LANES), BF),
            pltpu.VMEM((n_c, LANES), F32),
            pltpu.VMEM((1, width), F32),
            pltpu.VMEM((ns // m, tok_len, group_w + LANES), BF),
            pltpu.VMEM((ns, tok_len, group_w + LANES), BF),
            pltpu.VMEM((nx, 1, group_w), F32),
            pltpu.VMEM((ns, 1, group_w), F32),
            pltpu.VMEM((group_w, block), BF),
            pltpu.VMEM((m, 2 * buckets, LANES), BF),
            pltpu.VMEM((2 * buckets, group_w), BF),
            pltpu.VMEM((ns, tok_len, block), F32),
            pltpu.VMEM((ns, tok_len, block), F32),
            pltpu.VMEM((ns, 2, block), F32),
            pltpu.VMEM((ns, 2, block), F32),
            pltpu.VMEM((tok_len, kv_w), F32),
            stat,
            stat,
            stat,
            pltpu.VMEM((slot, LANES), F32),
            pltpu.VMEM((heads, LANES), F32),
            pltpu.VMEM((2 * heads, LANES), F32),
            pltpu.VMEM((2 * heads, LANES), F32),
            pltpu.VMEM((slot, LANES), BF),
            pltpu.VMEM((ns, slot, LANES), BF),
            pltpu.VMEM((ns, slot, LANES), F32),
            pltpu.VMEM((ns, LANES), BF),
            pltpu.VMEM((zs, ns, LANES), BF),
            pltpu.SemaphoreType.DMA((6,)),
            pltpu.SemaphoreType.DMA((10,)),
            pltpu.SemaphoreType.DMA((10,)),
        ],
        compiler_params=pltpu.CompilerParams(collective_id=0, has_side_effects=True),
    )(
        concept_ids,
        positions,
        timesteps,
        txt_tokens[0],
        counts[None, :],
        mod_table,
        kv_bias[None, :],
        key_gain[None, :],
        concept_table,
        kv_weight,
        img_query[0],
        img_key[0],
        img_value[0],
        out_grad[0],
    )
    return grad_t.T


def solution(mesh):
    placed = (
        P(("dp", "fsdp"), None, None),
        P("dp", None),
        P(("dp", "fsdp")),
        P(("dp", "fsdp")),
        P(("dp", "fsdp")),
        P("dp"),
        P(None, None, "fsdp"),
        P("fsdp", None),
        P(),
        P(),
        P(("dp", "fsdp"), None, None),
        P(("dp", "fsdp"), None, None),
        P(("dp", "fsdp"), None, None),
        P(("dp", "fsdp"), None, None),
    )
    return jax.shard_map(
        shards, mesh=mesh, in_specs=placed, out_specs=P("dp", "fsdp"), check_vma=False
    )
```

```python
import functools
import jax
import jax.numpy as jnp
from jax import lax
from jax.experimental import pallas as pl
from jax.experimental.pallas import tpu as pltpu
from jax.sharding import PartitionSpec as P

EPSILON = 1e-06
LANES = 128
BF = jnp.bfloat16
F32 = jnp.float32
MESH = pl.DeviceIdType.MESH
NT_DIMS = (((1,), (1,)), ((), ()))
TN_DIMS = (((0,), (0,)), ((), ()))


def split_two(values):
    high = values.astype(BF)
    low = (values - high.astype(F32)).astype(BF)
    return high, low


def iota(shape, axis):
    return lax.broadcasted_iota(jnp.int32, shape, axis)


def far_first(sizes):
    steps = [(a, b, c) for a in range(sizes[0]) for b in range(sizes[1]) for c in range(2)]

    def hops(step):
        return sum(min(d, n - d) for d, n in zip(step[:2], sizes))

    return sorted(steps[1:], key=lambda step: (-hops(step), step))


def step_kernel(
    dims,
    ids_s,
    pos_s,
    time_s,
    tok_any,
    counts_any,
    mods_any,
    bias_any,
    gain_any,
    table_any,
    weight_any,
    q_any,
    k_any,
    v_any,
    g_any,
    out,
    tok,
    counts,
    mods,
    bias,
    gain,
    table,
    weight,
    q,
    k,
    v,
    g,
    mod32,
    modp,
    lab_own,
    lab_recv,
    idz_own,
    idz_recv,
    belongs_a,
    belongs_b,
    id_buf,
    id_own,
    row32,
    row_send,
    row_recv,
    c32,
    c_row,
    cut_a,
    cut_b,
    tok_msg,
    tok_recv,
    c_msg,
    c_recv,
    w_t,
    w_recv,
    mod_recv,
    part,
    part_recv,
    late,
    late_recv,
    kv,
    m_img,
    l_img,
    d_img,
    dkv32,
    raw32,
    s1_32,
    s2_32,
    dkv_own,
    dkv_recv,
    dkv_wide,
    g32,
    g_own,
    g_recv,
    load_sem,
    send_sem,
    recv_sem,
):
    zs, nx, ny = dims
    ns = nx * ny * 2
    m = ny * 2
    z = lax.axis_index("dp")
    f = lax.axis_index("fsdp")
    groups = nx
    my_x = lax.div(f, m)
    my_y = lax.div(lax.rem(f, m), 2)
    my_c = lax.rem(f, 2)
    tok_len, width = tok.shape
    slice_w = weight.shape[0]
    kv_w = weight.shape[1]
    head_w = kv_w // 2
    heads = head_w // LANES
    block = kv_w // m
    group_w = slice_w * m
    n_img = q.shape[0]
    rows_own = table.shape[0]
    buckets = mods.shape[0]
    inv_root = 1.0 / (LANES**0.5)

    x_at = [lax.rem(my_x + d, nx) for d in range(nx)]
    y_at = [lax.rem(my_y + d, ny) for d in range(ny)]
    c_at = [my_c, 1 - my_c]
    chips = nx * ny
    plane = [
        ((x_at[a] * ny + y_at[b]) * 2 + c_at[c], c_at[c] * chips + x_at[a] * ny + y_at[b])
        for a, b, c in far_first((nx, ny))
    ]
    same_core = [
        ((x_at[a] * ny + y_at[b]) * 2 + my_c, x_at[a] * ny + y_at[b])
        for a, b, c in far_first((nx, ny))
        if c == 0
    ]
    chip_of = [x_at[a] * ny + y_at[b] for a, b, c in far_first((nx, ny))]
    me_chip = my_x * ny + my_y
    me = my_c * chips + me_chip
    from_me = my_x * m + lax.rem(my_x + my_y, ny) * 2 + my_c
    ring = my_x * (1 - my_c) + my_y * my_c
    own_slot = my_c * nx + ring
    own_block = lax.rem(my_x + my_y, ny) * 2 + my_c
    mates = []
    for b, c in sorted(
        ((b, c) for b in range(ny) for c in range(2)), key=lambda bc: -min(bc[0], ny - bc[0])
    ):
        if b or c:
            mate_x = lax.rem(my_x + b * (1 - my_c), nx)
            mate_y = lax.rem(my_y + b * my_c, ny)
            mates.append(
                (
                    (mate_x * ny + mate_y) * 2 + c_at[c],
                    lax.rem(mate_x + mate_y, ny) * 2 + c_at[c],
                )
            )
    line = [
        lax.rem(z + d, zs) for d in sorted(range(1, zs), key=lambda d: (-min(d, zs - d), d))
    ]

    barrier = pltpu.get_barrier_semaphore()
    for peer in line:
        pl.semaphore_signal(barrier, inc=1, device_id=(peer, f), device_id_type=MESH)

    pairs = (
        (tok_any, tok),
        (mods_any, mods),
        (weight_any, weight),
        (q_any, q),
        (k_any, k),
        (v_any, v),
        (g_any, g),
        (table_any, table),
        (counts_any, counts),
        (bias_any, bias),
        (gain_any, gain),
    )
    loads = [
        pltpu.make_async_copy(src, dst, load_sem.at[i]) for i, (src, dst) in enumerate(pairs)
    ]
    for copy in loads:
        copy.start()

    for peer, _ in plane:
        pl.semaphore_signal(barrier, inc=1, device_id=(z, peer), device_id_type=MESH)

    own_id = ids_s[0]
    own_pos = pos_s[0]
    own_time = time_s[0]
    id_own[...] = jnp.full(id_own.shape, own_id, jnp.int32)
    id_buf[z] = id_own[...]

    lane = iota((1, LANES), 1)
    label = jnp.where(lane == 0, own_time, jnp.where(lane == 1, own_pos, own_id))
    lab_own[...] = label.astype(F32)
    lab_recv[me] = lab_own[...]
    at_pos = iota((tok_len, 1), 0) == own_pos

    loads[0].wait()
    tok_f = tok[...].astype(F32)
    centre = jnp.mean(tok_f, -1, keepdims=True)
    spread = jnp.mean((tok_f - centre) ** 2, -1, keepdims=True)
    tok_hat = ((tok_f - centre) * lax.rsqrt(spread + EPSILON)).astype(BF)
    half_w = nx * slice_w
    tok_32 = tok_hat.astype(F32)
    for a in range(nx):
        for b in range(ny):
            at = (a * ny + b) * 2 * slice_w
            cut_a[b, :, a * slice_w : (a + 1) * slice_w] = tok_32[:, at : at + slice_w]
            at += slice_w
            cut_b[a, :, b * slice_w : (b + 1) * slice_w] = tok_32[:, at : at + slice_w]
    for a in range(nx):
        for b in range(ny):
            tok_msg[a * ny + b, :, :half_w] = cut_a[b].astype(BF)
            tok_msg[a * ny + b, :, half_w:] = cut_b[a].astype(BF)
    tok_recv[my_c, me_chip] = tok_msg[me_chip]

    mod32[...] = jnp.zeros(mod32.shape, F32)
    loads[1].wait()
    mod32[:, :, :slice_w] = mods[...].astype(F32)
    modp[:buckets, :] = mod32[:, 0, :].astype(BF)
    modp[buckets:, :] = mod32[:, 1, :].astype(BF)
    mod_recv[own_slot] = modp[...]
    loads[2].wait()
    w_recv[pl.ds(pl.multiple_of(own_slot * slice_w, 16), slice_w), :] = weight[
        :, pl.ds(pl.multiple_of(own_block * block, LANES), block)
    ]

    pl.semaphore_wait(barrier, zs - 1 + ns - 1)

    def remote(src, dst, phase, device):
        return pltpu.make_async_remote_copy(
            src_ref=src,
            dst_ref=dst,
            send_sem=send_sem.at[phase],
            recv_sem=recv_sem.at[phase],
            device_id=device,
            device_id_type=MESH,
        )

    def finish(ref, phase):
        pltpu.make_async_copy(ref, ref, recv_sem.at[phase]).wait()

    def drain(ref, phase):
        pltpu.make_async_copy(ref, ref, send_sem.at[phase]).wait()

    for peer in line:
        remote(id_own, id_buf.at[z], 0, (peer, f)).start()

    for peer, _ in plane:
        remote(lab_own, lab_recv.at[me], 10, (z, peer)).start()

    for peer, chip in same_core:
        remote(tok_msg.at[chip], tok_recv.at[my_c, me_chip], 4, (z, peer)).start()

    for peer, _ in mates:
        remote(modp, mod_recv.at[own_slot], 2, (z, peer)).start()

    for peer, theirs in mates:
        remote(
            weight.at[:, pl.ds(pl.multiple_of(theirs * block, LANES), block)],
            w_recv.at[pl.ds(pl.multiple_of(own_slot * slice_w, 16), slice_w), :],
            1,
            (z, peer),
        ).start()

    for copy in loads[3:]:
        copy.wait()

    def image_head(h, c):
        lanes = pl.ds(pl.multiple_of(h * LANES, LANES), LANES)
        scores = (
            lax.dot_general(k[:, lanes], q[:, lanes], NT_DIMS, preferred_element_type=F32)
            * inv_root
        )
        grads = lax.dot_general(v[:, lanes], g[:, lanes], NT_DIMS, preferred_element_type=F32)
        top = jnp.max(scores, 0, keepdims=True)
        raised = jnp.exp(scores - top)
        m_img[h] = top
        l_img[h] = jnp.sum(raised, 0, keepdims=True)
        d_img[h] = jnp.sum(raised.astype(BF).astype(F32) * grads, 0, keepdims=True)
        return c

    half = heads // 2
    lax.fori_loop(0, half, image_head, 0)

    finish(id_buf.at[pl.ds(0, zs - 1)], 0)
    wanted = id_buf[:, 0, :][:, :1]
    pick = (iota((zs, rows_own), 1) + z * rows_own == wanted).astype(F32).astype(BF)
    rows = jnp.dot(pick, table[...], preferred_element_type=F32)
    for c in range(width // LANES):
        row32[:, c, :] = rows[:, c * LANES : (c + 1) * LANES]
    row_send[...] = row32[...].astype(BF)
    row_recv[z] = row_send[z]
    for peer in line:
        remote(row_send.at[peer], row_recv.at[z], 3, (peer, f)).start()

    finish(lab_recv.at[pl.ds(0, ns - 1)], 10)
    labels = lab_recv[:, 0, :]
    pick_s = (iota((ns, buckets), 1) == labels[:, 0:1].astype(jnp.int32)).astype(F32).astype(BF)
    scale_own = 1.0 + jnp.dot(pick_s, modp[buckets:, :], preferred_element_type=F32)

    sample_diag = iota((ns, LANES), 0) == iota((ns, LANES), 1)
    idz_own[...] = jnp.sum(jnp.where(sample_diag, labels[:, 2:3], 0.0), 0, keepdims=True)
    idz_recv[z] = idz_own[...]
    for peer in line:
        remote(idz_own, idz_recv.at[z], 11, (peer, f)).start()

    finish(tok_recv.at[0, pl.ds(0, chips - 1)], 4)
    remote(tok_recv.at[my_c], tok_recv.at[my_c], 12, (z, f + 1 - 2 * my_c)).start()

    lax.fori_loop(half, heads, image_head, 0)

    table_f = table[...].astype(F32)
    t_centre = jnp.mean(table_f, -1, keepdims=True)
    t_spread = jnp.mean((table_f - t_centre) ** 2, -1, keepdims=True)
    t_rstd = lax.rsqrt(t_spread + EPSILON)
    diag = iota((rows_own, rows_own), 0) == iota((rows_own, rows_own), 1)
    own_scale = jnp.sum(jnp.where(diag, t_rstd, 0.0), 0, keepdims=True) / counts[...].astype(F32)

    finish(mod_recv.at[pl.ds(0, m - 1)], 2)
    lane_row = iota((LANES, group_w), 0)
    lane_col = iota((LANES, group_w), 1)
    mod_sum = jnp.zeros((2 * buckets, group_w), F32)
    for c in range(m):
        place = ((lane_col == lane_row + c * slice_w) & (lane_row < slice_w)).astype(F32)
        mod_sum += jnp.dot(mod_recv[c], place.astype(BF), preferred_element_type=F32)
    shift_s = jnp.dot(pick_s, mod_sum[:buckets].astype(BF), preferred_element_type=F32)
    scale_s = 1.0 + jnp.dot(pick_s, mod_sum[buckets:].astype(BF), preferred_element_type=F32)

    finish(tok_recv.at[0], 12)
    toks = tok_recv[...].astype(F32).reshape(ns, tok_len, group_w)
    modulated = scale_s.reshape(ns, 1, group_w) * toks + shift_s.reshape(ns, 1, group_w)
    a_high, a_low = split_two(scale_s)
    placed = iota((ns, tok_len, 1), 1) == lab_recv[:, :, 1:2].astype(jnp.int32)
    finish(w_recv.at[pl.ds(0, (m - 1) * slice_w)], 1)
    terms = jnp.dot(
        modulated.reshape(ns * tok_len, group_w).astype(BF),
        w_recv[...],
        preferred_element_type=F32,
    )
    extra = jnp.dot(
        jnp.concatenate([a_high, a_low], 0), w_recv[...], preferred_element_type=F32
    )
    sums = (extra[:ns] + extra[ns:]).reshape(ns, 1, block)
    part[...] = jnp.where(placed, sums, terms.reshape(ns, tok_len, block))
    part_recv[from_me] = part[me]
    for peer, slot in plane:
        remote(part.at[slot], part_recv.at[from_me], 5, (z, peer)).start()

    finish(row_recv.at[pl.ds(0, zs - 1)], 3)
    concept = jnp.sum(row_recv[...].astype(F32), 0)
    c_mean = jnp.sum(jnp.sum(concept, -1, keepdims=True), 0, keepdims=True) / width
    c_diff = concept - c_mean
    c_var = jnp.sum(jnp.sum(c_diff * c_diff, -1, keepdims=True), 0, keepdims=True) / width
    c32[...] = (c_diff * lax.rsqrt(c_var + EPSILON)).astype(BF).astype(F32)
    for c in range(width // LANES):
        c_row[:, c * LANES : (c + 1) * LANES] = c32[c : c + 1, :]
    for a in range(nx):
        for b in range(ny):
            at = (a * ny + b) * 2 * slice_w
            cut_a[b, 0:1, a * slice_w : (a + 1) * slice_w] = c_row[:, at : at + slice_w]
            at += slice_w
            cut_b[a, 0:1, b * slice_w : (b + 1) * slice_w] = c_row[:, at : at + slice_w]
    for a in range(nx):
        for b in range(ny):
            c_msg[a * ny + b, :, :half_w] = cut_a[b, 0:1, :]
            c_msg[a * ny + b, :, half_w:] = cut_b[a, 0:1, :]
    c_recv[me] = c_msg[me_chip]
    for (peer, _), chip in zip(plane, chip_of):
        remote(c_msg.at[chip], c_recv.at[me], 9, (z, peer)).start()

    own_row = iota((group_w, LANES), 0)
    own_col = iota((group_w, LANES), 1)
    own_place = ((own_row == own_col + own_slot * slice_w) & (own_col < slice_w)).astype(F32).astype(BF)

    finish(c_recv.at[pl.ds(0, ns - 1)], 9)
    concepts = c_recv[:, 0, :]
    scaled = scale_s * concepts
    b_high, b_low = split_two(scaled)
    extra = jnp.dot(
        jnp.concatenate([(scaled + shift_s).astype(BF), b_high, b_low], 0),
        w_recv[...],
        preferred_element_type=F32,
    )
    late[:, 0, :] = extra[:ns]
    late[:, 1, :] = extra[ns : 2 * ns] + extra[2 * ns :]
    late_recv[from_me] = late[me]
    for peer, slot in plane:
        remote(late.at[slot], late_recv.at[from_me], 6, (z, peer)).start()
    concept_own = jnp.dot(concepts.astype(BF), own_place, preferred_element_type=F32)

    finish(idz_recv.at[pl.ds(0, zs - 1)], 11)
    id_cols = jnp.sum(
        jnp.where(sample_diag.reshape(1, ns, LANES), idz_recv[...], 0.0), -1, keepdims=True
    ).astype(jnp.int32)
    belongs = (iota((zs, ns, rows_own), 2) + z * rows_own == id_cols).astype(F32)
    half_n, quarter = ns // 2, ns // 4
    for c in range(2):
        belongs_a[:, c * rows_own : (c + 1) * rows_own] = (
            belongs[:, c * half_n : (c + 1) * half_n, :].reshape(zs * half_n, rows_own).astype(BF)
        )
    for c in range(4):
        belongs_b[:, c * rows_own : (c + 1) * rows_own] = (
            belongs[:, c * quarter : (c + 1) * quarter, :]
            .reshape(zs * quarter, rows_own)
            .astype(BF)
        )

    for c in range(2 * heads):
        lanes = slice(c * LANES, (c + 1) * LANES)
        w_t[lanes, :] = weight[:, lanes].astype(F32).T.astype(BF)

    finish(part_recv.at[pl.ds(0, ns - 1)], 5)
    finish(late_recv.at[pl.ds(0, ns - 1)], 6)
    per = block // LANES
    pos_f = at_pos.astype(F32)
    for c in range(m):
        total = part_recv[c]
        extras = late_recv[c]
        for a in range(1, groups):
            total += part_recv[a * m + c]
            extras += late_recv[a * m + c]
        first = jnp.sum(total * pos_f, 0, keepdims=True)
        kv[:, c * block : (c + 1) * block] = jnp.where(at_pos, extras[0:1, :], total)
        for b in range(per):
            s1_32[c * per + b : c * per + b + 1, :] = first[:, b * LANES : (b + 1) * LANES]
            s2_32[c * per + b : c * per + b + 1, :] = extras[1:2, b * LANES : (b + 1) * LANES]

    kv_all = kv[...] + bias[...]
    gains = gain[...]
    raw_row = jnp.sum(kv_all[:, :head_w] * pos_f, 0, keepdims=True)
    key_parts = []
    for h in range(heads):
        raw = kv_all[:, h * LANES : (h + 1) * LANES]
        inv = lax.rsqrt(jnp.mean(raw * raw, -1, keepdims=True) + EPSILON)
        key_parts.append((raw * inv * gains).astype(BF).astype(F32))
        raw32[h : h + 1, :] = raw_row[:, h * LANES : (h + 1) * LANES]
    key_txt = jnp.concatenate(key_parts, 1)
    val_txt = kv_all[:, head_w:].astype(BF).astype(F32)
    own_head = iota((heads * tok_len, head_w), 0) // tok_len == iota(
        (heads * tok_len, head_w), 1
    ) // LANES
    key_diag = jnp.where(own_head, jnp.concatenate([key_txt] * heads, 0), 0.0).astype(BF)
    val_diag = jnp.where(own_head, jnp.concatenate([val_txt] * heads, 0), 0.0).astype(BF)
    s_txt = (
        lax.dot_general(key_diag, q[...], NT_DIMS, preferred_element_type=F32) * inv_root
    ).reshape(heads, tok_len, n_img)
    g_txt = lax.dot_general(val_diag, g[...], NT_DIMS, preferred_element_type=F32).reshape(
        heads, tok_len, n_img
    )
    top_img = m_img[...]
    top = jnp.maximum(top_img, jnp.max(s_txt, 1, keepdims=True))
    raised = jnp.exp(s_txt - top)
    alpha = jnp.exp(top_img - top)
    denom = alpha * l_img[...] + jnp.sum(raised, 1, keepdims=True)
    probs = raised / denom
    delta = alpha * d_img[...] / denom + jnp.sum(
        probs.astype(BF).astype(F32) * g_txt, 1, keepdims=True
    )
    pos_3 = (iota((1, tok_len, 1), 1) == own_pos).astype(F32)
    p_pos = jnp.sum(probs * pos_3, 1)
    g_pos = jnp.sum(g_txt * pos_3, 1)
    d_score = p_pos * (g_pos - delta[:, 0, :]) * inv_root
    p_high, p_low = split_two(p_pos)
    d_high, d_low = split_two(d_score)
    d_val = jnp.dot(
        jnp.concatenate([p_high.astype(F32), p_low.astype(F32)], 0).astype(BF),
        g[...],
        preferred_element_type=F32,
    )
    d_key = jnp.dot(
        jnp.concatenate([d_high.astype(F32), d_low.astype(F32)], 0).astype(BF),
        q[...],
        preferred_element_type=F32,
    )
    d_val = d_val[:heads] + d_val[heads:]
    d_key = d_key[:heads] + d_key[heads:]
    dkv32[...] = jnp.zeros(dkv32.shape, F32)
    for h in range(heads):
        dkv32[h : h + 1, :] = d_key[h : h + 1, h * LANES : (h + 1) * LANES]
        dkv32[heads + h : heads + h + 1, :] = d_val[h : h + 1, h * LANES : (h + 1) * LANES]
    raw_pos = raw32[...]
    inv_pos = lax.rsqrt(jnp.mean(raw_pos * raw_pos, -1, keepdims=True) + EPSILON)
    n_pos = raw_pos * inv_pos
    d_norm = dkv32[:heads, :] * gains
    dkv32[:heads, :] = inv_pos * (d_norm - n_pos * jnp.mean(d_norm * n_pos, -1, keepdims=True))
    dkv_rows = dkv32[: 2 * heads, :].astype(BF).astype(F32)
    mean_1 = jnp.sum(jnp.sum(dkv_rows * s1_32[...], -1, keepdims=True), 0, keepdims=True) / width
    mean_2 = jnp.sum(jnp.sum(dkv_rows * s2_32[...], -1, keepdims=True), 0, keepdims=True) / width
    for c, value in enumerate((mean_1, mean_2)):
        high, low = split_two(value)
        at = 2 * heads + 2 * c
        dkv32[at : at + 1, :] = jnp.broadcast_to(high.astype(F32), (1, LANES))
        dkv32[at + 1 : at + 2, :] = jnp.broadcast_to(low.astype(F32), (1, LANES))
    dkv_own[...] = dkv32[...].astype(BF)
    dkv_recv[me] = dkv_own[...]

    for peer, _ in plane:
        remote(dkv_own, dkv_recv.at[me], 7, (z, peer)).start()
    finish(dkv_recv.at[pl.ds(0, ns - 1)], 7)
    dkv_wide[...] = dkv_recv[...].astype(F32)
    grads = jnp.zeros((ns, slice_w), F32)
    for c in range(0, 2 * heads, 2):
        both = jnp.concatenate([dkv_wide[:, c, :], dkv_wide[:, c + 1, :]], 1).astype(BF)
        grads += jnp.dot(
            both, w_t[c * LANES : (c + 2) * LANES, :], preferred_element_type=F32
        )
    at = 2 * heads
    mean_1 = (dkv_wide[:, at, :] + dkv_wide[:, at + 1, :])[:, :slice_w]
    mean_2 = (dkv_wide[:, at + 2, :] + dkv_wide[:, at + 3, :])[:, :slice_w]
    row_grad = grads * scale_own[:, :slice_w] - mean_1 - concept_own[:, :slice_w] * mean_2
    for c in range(2):
        g32[:half_n, c * 64 : c * 64 + 64] = row_grad[c * half_n : (c + 1) * half_n, :64]
    for c in range(4):
        g32[half_n:, c * 32 : c * 32 + 32] = row_grad[c * quarter : (c + 1) * quarter, 64:]
    g_own[...] = g32[...].astype(BF)
    g_recv[z] = g_own[...]

    for peer in line:
        remote(g_own, g_recv.at[z], 8, (peer, f)).start()
    finish(g_recv.at[pl.ds(0, zs - 1)], 8)
    wide = g_recv[...].astype(F32)
    sum_a = lax.dot_general(
        wide[:, :half_n, :].reshape(zs * half_n, LANES).astype(BF),
        belongs_a[...],
        TN_DIMS,
        preferred_element_type=F32,
    )
    sum_b = lax.dot_general(
        wide[:, half_n:, :].reshape(zs * quarter, LANES).astype(BF),
        belongs_b[...],
        TN_DIMS,
        preferred_element_type=F32,
    )
    top_rows = sum_a[:64, :rows_own] + sum_a[64:, rows_own:]
    low_rows = sum_b[:32, :rows_own]
    for c in range(1, 4):
        low_rows += sum_b[c * 32 : c * 32 + 32, c * rows_own : (c + 1) * rows_own]
    out[:64, :] = top_rows * own_scale
    out[64:, :] = low_rows * own_scale

    drain(id_buf.at[pl.ds(0, zs - 1)], 0)
    drain(w_recv.at[pl.ds(0, (m - 1) * slice_w)], 1)
    drain(mod_recv.at[pl.ds(0, m - 1)], 2)
    drain(row_recv.at[pl.ds(0, zs - 1)], 3)
    drain(tok_recv.at[0, pl.ds(0, chips - 1)], 4)
    drain(tok_recv.at[0], 12)
    drain(part_recv.at[pl.ds(0, ns - 1)], 5)
    drain(late_recv.at[pl.ds(0, ns - 1)], 6)
    drain(dkv_recv.at[pl.ds(0, ns - 1)], 7)
    drain(g_recv.at[pl.ds(0, zs - 1)], 8)
    drain(c_recv.at[pl.ds(0, ns - 1)], 9)
    drain(lab_recv.at[pl.ds(0, ns - 1)], 10)
    drain(idz_recv.at[pl.ds(0, zs - 1)], 11)


def shards(
    txt_tokens,
    concept_table,
    concept_ids,
    positions,
    timesteps,
    counts,
    mod_table,
    kv_weight,
    kv_bias,
    key_gain,
    img_query,
    img_key,
    img_value,
    out_grad,
):
    ns = lax.axis_size("fsdp")
    zs = lax.axis_size("dp")
    nx, ny = (4, 4) if ns == 32 else (2, 2)
    m = ny * 2
    tok_len, width = txt_tokens.shape[1:]
    slice_w, kv_w = kv_weight.shape
    head_w = kv_w // 2
    heads = head_w // LANES
    n_img = img_query.shape[1]
    buckets = mod_table.shape[0]
    rows_own = concept_table.shape[0]
    block = kv_w // m
    group_w = slice_w * m
    n_c = width // LANES
    slot = (2 * heads + 4 + 15) // 16 * 16

    vm = pl.BlockSpec(memory_space=pltpu.VMEM)
    sm = pl.BlockSpec(memory_space=pltpu.SMEM)
    hb = pl.BlockSpec(memory_space=pl.ANY)
    image = pltpu.VMEM((n_img, head_w), BF)
    stat = pltpu.VMEM((heads, 1, n_img), F32)
    grad_t = pl.pallas_call(
        functools.partial(step_kernel, (zs, nx, ny)),
        out_shape=jax.ShapeDtypeStruct((slice_w, rows_own), F32),
        in_specs=[sm] * 3 + [hb] * 11,
        out_specs=vm,
        scratch_shapes=[
            pltpu.VMEM((tok_len, width), BF),
            pltpu.VMEM((1, rows_own), jnp.int32),
            pltpu.VMEM((buckets, 2, slice_w), BF),
            pltpu.VMEM((1, kv_w), F32),
            pltpu.VMEM((1, LANES), F32),
            pltpu.VMEM((rows_own, width), BF),
            pltpu.VMEM((slice_w, kv_w), BF),
            image,
            image,
            image,
            image,
            pltpu.VMEM((buckets, 2, LANES), F32),
            pltpu.VMEM((2 * buckets, LANES), BF),
            pltpu.VMEM((1, LANES), F32),
            pltpu.VMEM((ns, 1, LANES), F32),
            pltpu.VMEM((1, LANES), F32),
            pltpu.VMEM((zs, 1, LANES), F32),
            pltpu.VMEM((zs * ns // 2, 2 * rows_own), BF),
            pltpu.VMEM((zs * ns // 4, 4 * rows_own), BF),
            pltpu.VMEM((zs, 1, LANES), jnp.int32),
            pltpu.VMEM((1, LANES), jnp.int32),
            pltpu.VMEM((zs, n_c, LANES), F32),
            pltpu.VMEM((zs, n_c, LANES), BF),
            pltpu.VMEM((zs, n_c, LANES), BF),
            pltpu.VMEM((n_c, LANES), F32),
            pltpu.VMEM((1, width), F32),
            pltpu.VMEM((ny, tok_len, nx * slice_w), F32),
            pltpu.VMEM((nx, tok_len, ny * slice_w), F32),
            pltpu.VMEM((nx * ny, tok_len, group_w), BF),
            pltpu.VMEM((2, nx * ny, tok_len, group_w), BF),
            pltpu.VMEM((nx * ny, 1, group_w), F32),
            pltpu.VMEM((ns, 1, group_w), F32),
            pltpu.VMEM((kv_w, slice_w), BF),
            pltpu.VMEM((group_w, block), BF),
            pltpu.VMEM((m, 2 * buckets, LANES), BF),
            pltpu.VMEM((ns, tok_len, block), F32),
            pltpu.VMEM((ns, tok_len, block), F32),
            pltpu.VMEM((ns, 2, block), F32),
            pltpu.VMEM((ns, 2, block), F32),
            pltpu.VMEM((tok_len, kv_w), F32),
            stat,
            stat,
            stat,
            pltpu.VMEM((slot, LANES), F32),
            pltpu.VMEM((heads, LANES), F32),
            pltpu.VMEM((2 * heads, LANES), F32),
            pltpu.VMEM((2 * heads, LANES), F32),
            pltpu.VMEM((slot, LANES), BF),
            pltpu.VMEM((ns, slot, LANES), BF),
            pltpu.VMEM((ns, slot, LANES), F32),
            pltpu.VMEM((ns * 3 // 4, LANES), F32),
            pltpu.VMEM((ns * 3 // 4, LANES), BF),
            pltpu.VMEM((zs, ns * 3 // 4, LANES), BF),
            pltpu.SemaphoreType.DMA((11,)),
            pltpu.SemaphoreType.DMA((13,)),
            pltpu.SemaphoreType.DMA((13,)),
        ],
        compiler_params=pltpu.CompilerParams(collective_id=0, has_side_effects=True),
    )(
        concept_ids,
        positions,
        timesteps,
        txt_tokens[0],
        counts[None, :],
        mod_table,
        kv_bias[None, :],
        key_gain[None, :],
        concept_table,
        kv_weight,
        img_query[0],
        img_key[0],
        img_value[0],
        out_grad[0],
    )
    return grad_t.T


def solution(mesh):
    placed = (
        P(("dp", "fsdp"), None, None),
        P("dp", None),
        P(("dp", "fsdp")),
        P(("dp", "fsdp")),
        P(("dp", "fsdp")),
        P("dp"),
        P(None, None, "fsdp"),
        P("fsdp", None),
        P(),
        P(),
        P(("dp", "fsdp"), None, None),
        P(("dp", "fsdp"), None, None),
        P(("dp", "fsdp"), None, None),
        P(("dp", "fsdp"), None, None),
    )
    return jax.shard_map(
        shards, mesh=mesh, in_specs=placed, out_specs=P("dp", "fsdp"), check_vma=False
    )
```

```python
import functools
import jax
import jax.numpy as jnp
from jax import lax
from jax.experimental import pallas as pl
from jax.experimental.pallas import tpu as pltpu
from jax.sharding import PartitionSpec as P

EPSILON = 1e-06
LANES = 128
BF = jnp.bfloat16
F32 = jnp.float32
MESH = pl.DeviceIdType.MESH
NT_DIMS = (((1,), (1,)), ((), ()))
TN_DIMS = (((0,), (0,)), ((), ()))


def split_two(values):
    high = values.astype(BF)
    low = (values - high.astype(F32)).astype(BF)
    return high, low


def iota(shape, axis):
    return lax.broadcasted_iota(jnp.int32, shape, axis)


def far_first(sizes):
    steps = [(a, b, c) for a in range(sizes[0]) for b in range(sizes[1]) for c in range(2)]

    def hops(step):
        return sum(min(d, n - d) for d, n in zip(step[:2], sizes))

    return sorted(steps[1:], key=lambda step: (-hops(step), step))


def step_kernel(
    dims,
    ids_s,
    pos_s,
    time_s,
    tok_any,
    counts_any,
    mods_any,
    bias_any,
    gain_any,
    table_any,
    weight_any,
    q_any,
    k_any,
    v_any,
    g_any,
    g_recv,
    belongs_a,
    belongs_b,
    meta,
    tok,
    counts,
    mods,
    bias,
    gain,
    table,
    weight,
    q,
    k,
    v,
    g,
    mod32,
    modp,
    lab_own,
    lab_recv,
    idz_own,
    idz_recv,
    id_buf,
    id_own,
    row32,
    row_send,
    row_recv,
    c32,
    c_row,
    cut_a,
    cut_b,
    tok_msg,
    tok_recv,
    c_msg,
    c_recv,
    w_t,
    w_recv,
    mod_recv,
    part,
    part_recv,
    late,
    late_recv,
    kv,
    m_img,
    l_img,
    d_img,
    dkv32,
    raw32,
    s1_32,
    s2_32,
    dkv_own,
    dkv_recv,
    dkv_wide,
    g32,
    g_own,
    load_sem,
    send_sem,
    recv_sem,
):
    zs, nx, ny = dims
    ns = nx * ny * 2
    m = ny * 2
    z = lax.axis_index("dp")
    f = lax.axis_index("fsdp")
    groups = nx
    my_x = lax.div(f, m)
    my_y = lax.div(lax.rem(f, m), 2)
    my_c = lax.rem(f, 2)
    tok_len, width = tok.shape
    slice_w = weight.shape[0]
    kv_w = weight.shape[1]
    head_w = kv_w // 2
    heads = head_w // LANES
    block = kv_w // m
    group_w = slice_w * m
    n_img = q.shape[0]
    rows_own = table.shape[0]
    buckets = mods.shape[0]
    inv_root = 1.0 / (LANES**0.5)

    x_at = [lax.rem(my_x + d, nx) for d in range(nx)]
    y_at = [lax.rem(my_y + d, ny) for d in range(ny)]
    c_at = [my_c, 1 - my_c]
    chips = nx * ny
    plane = [
        ((x_at[a] * ny + y_at[b]) * 2 + c_at[c], c_at[c] * chips + x_at[a] * ny + y_at[b])
        for a, b, c in far_first((nx, ny))
    ]
    same_core = [
        ((x_at[a] * ny + y_at[b]) * 2 + my_c, x_at[a] * ny + y_at[b])
        for a, b, c in far_first((nx, ny))
        if c == 0
    ]
    chip_of = [x_at[a] * ny + y_at[b] for a, b, c in far_first((nx, ny))]
    me_chip = my_x * ny + my_y
    me = my_c * chips + me_chip
    from_me = my_x * m + lax.rem(my_x + my_y, ny) * 2 + my_c
    ring = my_x * (1 - my_c) + my_y * my_c
    own_slot = my_c * nx + ring
    own_block = lax.rem(my_x + my_y, ny) * 2 + my_c
    mates = []
    for b, c in sorted(
        ((b, c) for b in range(ny) for c in range(2)), key=lambda bc: -min(bc[0], ny - bc[0])
    ):
        if b or c:
            mate_x = lax.rem(my_x + b * (1 - my_c), nx)
            mate_y = lax.rem(my_y + b * my_c, ny)
            mates.append(
                (
                    (mate_x * ny + mate_y) * 2 + c_at[c],
                    lax.rem(mate_x + mate_y, ny) * 2 + c_at[c],
                )
            )
    line = [
        lax.rem(z + d, zs) for d in sorted(range(1, zs), key=lambda d: (-min(d, zs - d), d))
    ]

    barrier = pltpu.get_barrier_semaphore()
    for peer in line:
        pl.semaphore_signal(barrier, inc=1, device_id=(peer, f), device_id_type=MESH)

    pairs = (
        (tok_any, tok),
        (mods_any, mods),
        (weight_any, weight),
        (q_any, q),
        (k_any, k),
        (v_any, v),
        (g_any, g),
        (table_any, table),
        (counts_any, counts),
        (bias_any, bias),
        (gain_any, gain),
    )
    loads = [
        pltpu.make_async_copy(src, dst, load_sem.at[i]) for i, (src, dst) in enumerate(pairs)
    ]
    for copy in loads:
        copy.start()

    for peer, _ in plane:
        pl.semaphore_signal(barrier, inc=1, device_id=(z, peer), device_id_type=MESH)

    own_id = ids_s[0]
    own_pos = pos_s[0]
    own_time = time_s[0]
    id_own[...] = jnp.full(id_own.shape, own_id, jnp.int32)
    id_buf[z] = id_own[...]

    lane = iota((1, LANES), 1)
    label = jnp.where(lane == 0, own_time, jnp.where(lane == 1, own_pos, own_id))
    lab_own[...] = label.astype(F32)
    lab_recv[me] = lab_own[...]
    at_pos = iota((tok_len, 1), 0) == own_pos

    loads[0].wait()
    tok_f = tok[...].astype(F32)
    centre = jnp.mean(tok_f, -1, keepdims=True)
    spread = jnp.mean((tok_f - centre) ** 2, -1, keepdims=True)
    tok_hat = ((tok_f - centre) * lax.rsqrt(spread + EPSILON)).astype(BF)
    half_w = nx * slice_w
    tok_32 = tok_hat.astype(F32)
    for a in range(nx):
        for b in range(ny):
            at = (a * ny + b) * 2 * slice_w
            cut_a[b, :, a * slice_w : (a + 1) * slice_w] = tok_32[:, at : at + slice_w]
            at += slice_w
            cut_b[a, :, b * slice_w : (b + 1) * slice_w] = tok_32[:, at : at + slice_w]
    for a in range(nx):
        for b in range(ny):
            tok_msg[a * ny + b, :, :half_w] = cut_a[b].astype(BF)
            tok_msg[a * ny + b, :, half_w:] = cut_b[a].astype(BF)
    tok_recv[my_c, me_chip] = tok_msg[me_chip]

    mod32[...] = jnp.zeros(mod32.shape, F32)
    loads[1].wait()
    mod32[:, :, :slice_w] = mods[...].astype(F32)
    modp[:buckets, :] = mod32[:, 0, :].astype(BF)
    modp[buckets:, :] = mod32[:, 1, :].astype(BF)
    mod_recv[own_slot] = modp[...]
    loads[2].wait()
    w_recv[pl.ds(pl.multiple_of(own_slot * slice_w, 16), slice_w), :] = weight[
        :, pl.ds(pl.multiple_of(own_block * block, LANES), block)
    ]

    pl.semaphore_wait(barrier, zs - 1 + ns - 1)

    def remote(src, dst, phase, device):
        return pltpu.make_async_remote_copy(
            src_ref=src,
            dst_ref=dst,
            send_sem=send_sem.at[phase],
            recv_sem=recv_sem.at[phase],
            device_id=device,
            device_id_type=MESH,
        )

    def finish(ref, phase):
        pltpu.make_async_copy(ref, ref, recv_sem.at[phase]).wait()

    def drain(ref, phase):
        pltpu.make_async_copy(ref, ref, send_sem.at[phase]).wait()

    for peer in line:
        remote(id_own, id_buf.at[z], 0, (peer, f)).start()

    for peer, _ in plane:
        remote(lab_own, lab_recv.at[me], 10, (z, peer)).start()

    for peer, chip in same_core:
        remote(tok_msg.at[chip], tok_recv.at[my_c, me_chip], 4, (z, peer)).start()

    for peer, _ in mates:
        remote(modp, mod_recv.at[own_slot], 2, (z, peer)).start()

    for peer, theirs in mates:
        remote(
            weight.at[:, pl.ds(pl.multiple_of(theirs * block, LANES), block)],
            w_recv.at[pl.ds(pl.multiple_of(own_slot * slice_w, 16), slice_w), :],
            1,
            (z, peer),
        ).start()

    for copy in loads[3:]:
        copy.wait()

    def image_head(h, c):
        lanes = pl.ds(pl.multiple_of(h * LANES, LANES), LANES)
        scores = (
            lax.dot_general(k[:, lanes], q[:, lanes], NT_DIMS, preferred_element_type=F32)
            * inv_root
        )
        grads = lax.dot_general(v[:, lanes], g[:, lanes], NT_DIMS, preferred_element_type=F32)
        top = jnp.max(scores, 0, keepdims=True)
        raised = jnp.exp(scores - top)
        m_img[h] = top
        l_img[h] = jnp.sum(raised, 0, keepdims=True)
        d_img[h] = jnp.sum(raised.astype(BF).astype(F32) * grads, 0, keepdims=True)
        return c

    half = heads // 2
    lax.fori_loop(0, half, image_head, 0)

    finish(id_buf.at[pl.ds(0, zs - 1)], 0)
    wanted = id_buf[:, 0, :][:, :1]
    pick = (iota((zs, rows_own), 1) + z * rows_own == wanted).astype(F32).astype(BF)
    rows = jnp.dot(pick, table[...], preferred_element_type=F32)
    for c in range(width // LANES):
        row32[:, c, :] = rows[:, c * LANES : (c + 1) * LANES]
    row_send[...] = row32[...].astype(BF)
    row_recv[z] = row_send[z]
    for peer in line:
        remote(row_send.at[peer], row_recv.at[z], 3, (peer, f)).start()

    finish(lab_recv.at[pl.ds(0, ns - 1)], 10)
    labels = lab_recv[:, 0, :]
    pick_s = (iota((ns, buckets), 1) == labels[:, 0:1].astype(jnp.int32)).astype(F32).astype(BF)
    scale_own = 1.0 + jnp.dot(pick_s, modp[buckets:, :], preferred_element_type=F32)

    sample_diag = iota((ns, LANES), 0) == iota((ns, LANES), 1)
    idz_own[...] = jnp.sum(jnp.where(sample_diag, labels[:, 2:3], 0.0), 0, keepdims=True)
    idz_recv[z] = idz_own[...]
    for peer in line:
        remote(idz_own, idz_recv.at[z], 11, (peer, f)).start()

    finish(tok_recv.at[0, pl.ds(0, chips - 1)], 4)
    remote(tok_recv.at[my_c], tok_recv.at[my_c], 12, (z, f + 1 - 2 * my_c)).start()

    finish(mod_recv.at[pl.ds(0, m - 1)], 2)
    lane_row = iota((LANES, group_w), 0)
    lane_col = iota((LANES, group_w), 1)
    mod_sum = jnp.zeros((2 * buckets, group_w), F32)
    for c in range(m):
        place = ((lane_col == lane_row + c * slice_w) & (lane_row < slice_w)).astype(F32)
        mod_sum += jnp.dot(mod_recv[c], place.astype(BF), preferred_element_type=F32)
    shift_s = jnp.dot(pick_s, mod_sum[:buckets].astype(BF), preferred_element_type=F32)
    scale_s = 1.0 + jnp.dot(pick_s, mod_sum[buckets:].astype(BF), preferred_element_type=F32)

    finish(tok_recv.at[0], 12)
    toks = tok_recv[...].astype(F32).reshape(ns, tok_len, group_w)
    modulated = scale_s.reshape(ns, 1, group_w) * toks + shift_s.reshape(ns, 1, group_w)
    a_high, a_low = split_two(scale_s)
    placed = iota((ns, tok_len, 1), 1) == lab_recv[:, :, 1:2].astype(jnp.int32)
    finish(w_recv.at[pl.ds(0, (m - 1) * slice_w)], 1)
    terms = jnp.dot(
        modulated.reshape(ns * tok_len, group_w).astype(BF),
        w_recv[...],
        preferred_element_type=F32,
    )
    extra = jnp.dot(
        jnp.concatenate([a_high, a_low], 0), w_recv[...], preferred_element_type=F32
    )
    sums = (extra[:ns] + extra[ns:]).reshape(ns, 1, block)
    part[...] = jnp.where(placed, sums, terms.reshape(ns, tok_len, block))
    part_recv[from_me] = part[me]
    for peer, slot in plane:
        remote(part.at[slot], part_recv.at[from_me], 5, (z, peer)).start()

    lax.fori_loop(half, heads, image_head, 0)

    table_f = table[...].astype(F32)
    t_centre = jnp.mean(table_f, -1, keepdims=True)
    t_spread = jnp.mean((table_f - t_centre) ** 2, -1, keepdims=True)
    t_rstd = lax.rsqrt(t_spread + EPSILON)
    diag = iota((rows_own, rows_own), 0) == iota((rows_own, rows_own), 1)
    meta[...] = jnp.sum(jnp.where(diag, t_rstd, 0.0), 0, keepdims=True) / counts[...].astype(F32)

    finish(row_recv.at[pl.ds(0, zs - 1)], 3)
    concept = jnp.sum(row_recv[...].astype(F32), 0)
    c_mean = jnp.sum(jnp.sum(concept, -1, keepdims=True), 0, keepdims=True) / width
    c_diff = concept - c_mean
    c_var = jnp.sum(jnp.sum(c_diff * c_diff, -1, keepdims=True), 0, keepdims=True) / width
    c32[...] = (c_diff * lax.rsqrt(c_var + EPSILON)).astype(BF).astype(F32)
    for c in range(width // LANES):
        c_row[:, c * LANES : (c + 1) * LANES] = c32[c : c + 1, :]
    for a in range(nx):
        for b in range(ny):
            at = (a * ny + b) * 2 * slice_w
            cut_a[b, 0:1, a * slice_w : (a + 1) * slice_w] = c_row[:, at : at + slice_w]
            at += slice_w
            cut_b[a, 0:1, b * slice_w : (b + 1) * slice_w] = c_row[:, at : at + slice_w]
    for a in range(nx):
        for b in range(ny):
            c_msg[a * ny + b, :, :half_w] = cut_a[b, 0:1, :]
            c_msg[a * ny + b, :, half_w:] = cut_b[a, 0:1, :]
    c_recv[me] = c_msg[me_chip]
    for (peer, _), chip in zip(plane, chip_of):
        remote(c_msg.at[chip], c_recv.at[me], 9, (z, peer)).start()

    own_row = iota((group_w, LANES), 0)
    own_col = iota((group_w, LANES), 1)
    own_place = ((own_row == own_col + own_slot * slice_w) & (own_col < slice_w)).astype(F32).astype(BF)

    finish(c_recv.at[pl.ds(0, ns - 1)], 9)
    concepts = c_recv[:, 0, :]
    scaled = scale_s * concepts
    b_high, b_low = split_two(scaled)
    extra = jnp.dot(
        jnp.concatenate([(scaled + shift_s).astype(BF), b_high, b_low], 0),
        w_recv[...],
        preferred_element_type=F32,
    )
    late[:, 0, :] = extra[:ns]
    late[:, 1, :] = extra[ns : 2 * ns] + extra[2 * ns :]
    late_recv[from_me] = late[me]
    for peer, slot in plane:
        remote(late.at[slot], late_recv.at[from_me], 6, (z, peer)).start()
    concept_own = jnp.dot(concepts.astype(BF), own_place, preferred_element_type=F32)

    finish(idz_recv.at[pl.ds(0, zs - 1)], 11)
    half_n, quarter = ns // 2, ns // 4
    id_cols = jnp.sum(
        jnp.where(sample_diag.reshape(1, ns, LANES), idz_recv[...], 0.0), -1, keepdims=True
    ).astype(jnp.int32)
    belongs = (iota((zs, ns, rows_own), 2) + z * rows_own == id_cols).astype(F32)
    for c in range(2):
        belongs_a[:, c * rows_own : (c + 1) * rows_own] = (
            belongs[:, c * half_n : (c + 1) * half_n, :].reshape(zs * half_n, rows_own).astype(BF)
        )
    for c in range(4):
        belongs_b[:, c * rows_own : (c + 1) * rows_own] = (
            belongs[:, c * quarter : (c + 1) * quarter, :]
            .reshape(zs * quarter, rows_own)
            .astype(BF)
        )

    for c in range(2 * heads):
        lanes = slice(c * LANES, (c + 1) * LANES)
        w_t[lanes, :] = weight[:, lanes].astype(F32).T.astype(BF)

    finish(part_recv.at[pl.ds(0, ns - 1)], 5)
    finish(late_recv.at[pl.ds(0, ns - 1)], 6)
    per = block // LANES
    pos_f = at_pos.astype(F32)
    for c in range(m):
        total = part_recv[c]
        extras = late_recv[c]
        for a in range(1, groups):
            total += part_recv[a * m + c]
            extras += late_recv[a * m + c]
        first = jnp.sum(total * pos_f, 0, keepdims=True)
        kv[:, c * block : (c + 1) * block] = jnp.where(at_pos, extras[0:1, :], total)
        for b in range(per):
            s1_32[c * per + b : c * per + b + 1, :] = first[:, b * LANES : (b + 1) * LANES]
            s2_32[c * per + b : c * per + b + 1, :] = extras[1:2, b * LANES : (b + 1) * LANES]

    kv_all = kv[...] + bias[...]
    gains = gain[...]
    raw_row = jnp.sum(kv_all[:, :head_w] * pos_f, 0, keepdims=True)
    key_parts = []
    for h in range(heads):
        raw = kv_all[:, h * LANES : (h + 1) * LANES]
        inv = lax.rsqrt(jnp.mean(raw * raw, -1, keepdims=True) + EPSILON)
        key_parts.append((raw * inv * gains).astype(BF).astype(F32))
        raw32[h : h + 1, :] = raw_row[:, h * LANES : (h + 1) * LANES]
    key_txt = jnp.concatenate(key_parts, 1)
    val_txt = kv_all[:, head_w:].astype(BF).astype(F32)
    own_head = iota((heads * tok_len, head_w), 0) // tok_len == iota(
        (heads * tok_len, head_w), 1
    ) // LANES
    key_diag = jnp.where(own_head, jnp.concatenate([key_txt] * heads, 0), 0.0).astype(BF)
    val_diag = jnp.where(own_head, jnp.concatenate([val_txt] * heads, 0), 0.0).astype(BF)
    s_txt = (
        lax.dot_general(key_diag, q[...], NT_DIMS, preferred_element_type=F32) * inv_root
    ).reshape(heads, tok_len, n_img)
    g_txt = lax.dot_general(val_diag, g[...], NT_DIMS, preferred_element_type=F32).reshape(
        heads, tok_len, n_img
    )
    top_img = m_img[...]
    top = jnp.maximum(top_img, jnp.max(s_txt, 1, keepdims=True))
    raised = jnp.exp(s_txt - top)
    alpha = jnp.exp(top_img - top)
    denom = alpha * l_img[...] + jnp.sum(raised, 1, keepdims=True)
    probs = raised / denom
    delta = alpha * d_img[...] / denom + jnp.sum(
        probs.astype(BF).astype(F32) * g_txt, 1, keepdims=True
    )
    pos_3 = (iota((1, tok_len, 1), 1) == own_pos).astype(F32)
    p_pos = jnp.sum(probs * pos_3, 1)
    g_pos = jnp.sum(g_txt * pos_3, 1)
    d_score = p_pos * (g_pos - delta[:, 0, :]) * inv_root
    p_high, p_low = split_two(p_pos)
    d_high, d_low = split_two(d_score)
    d_val = jnp.dot(
        jnp.concatenate([p_high.astype(F32), p_low.astype(F32)], 0).astype(BF),
        g[...],
        preferred_element_type=F32,
    )
    d_key = jnp.dot(
        jnp.concatenate([d_high.astype(F32), d_low.astype(F32)], 0).astype(BF),
        q[...],
        preferred_element_type=F32,
    )
    d_val = d_val[:heads] + d_val[heads:]
    d_key = d_key[:heads] + d_key[heads:]
    dkv32[...] = jnp.zeros(dkv32.shape, F32)
    for h in range(heads):
        dkv32[h : h + 1, :] = d_key[h : h + 1, h * LANES : (h + 1) * LANES]
        dkv32[heads + h : heads + h + 1, :] = d_val[h : h + 1, h * LANES : (h + 1) * LANES]
    raw_pos = raw32[...]
    inv_pos = lax.rsqrt(jnp.mean(raw_pos * raw_pos, -1, keepdims=True) + EPSILON)
    n_pos = raw_pos * inv_pos
    d_norm = dkv32[:heads, :] * gains
    dkv32[:heads, :] = inv_pos * (d_norm - n_pos * jnp.mean(d_norm * n_pos, -1, keepdims=True))
    dkv_rows = dkv32[: 2 * heads, :].astype(BF).astype(F32)
    mean_1 = jnp.sum(jnp.sum(dkv_rows * s1_32[...], -1, keepdims=True), 0, keepdims=True) / width
    mean_2 = jnp.sum(jnp.sum(dkv_rows * s2_32[...], -1, keepdims=True), 0, keepdims=True) / width
    for c, value in enumerate((mean_1, mean_2)):
        high, low = split_two(value)
        at = 2 * heads + 2 * c
        dkv32[at : at + 1, :] = jnp.broadcast_to(high.astype(F32), (1, LANES))
        dkv32[at + 1 : at + 2, :] = jnp.broadcast_to(low.astype(F32), (1, LANES))
    dkv_own[...] = dkv32[...].astype(BF)
    dkv_recv[me] = dkv_own[...]

    for peer, _ in plane:
        remote(dkv_own, dkv_recv.at[me], 7, (z, peer)).start()
    finish(dkv_recv.at[pl.ds(0, ns - 1)], 7)
    dkv_wide[...] = dkv_recv[...].astype(F32)
    grads = jnp.zeros((ns, slice_w), F32)
    for c in range(0, 2 * heads, 2):
        both = jnp.concatenate([dkv_wide[:, c, :], dkv_wide[:, c + 1, :]], 1).astype(BF)
        grads += jnp.dot(
            both, w_t[c * LANES : (c + 2) * LANES, :], preferred_element_type=F32
        )
    at = 2 * heads
    mean_1 = (dkv_wide[:, at, :] + dkv_wide[:, at + 1, :])[:, :slice_w]
    mean_2 = (dkv_wide[:, at + 2, :] + dkv_wide[:, at + 3, :])[:, :slice_w]
    row_grad = grads * scale_own[:, :slice_w] - mean_1 - concept_own[:, :slice_w] * mean_2
    for c in range(2):
        g32[:half_n, c * 64 : c * 64 + 64] = row_grad[c * half_n : (c + 1) * half_n, :64]
    for c in range(4):
        g32[half_n:, c * 32 : c * 32 + 32] = row_grad[c * quarter : (c + 1) * quarter, 64:]
    g_own[...] = g32[...].astype(BF)
    g_recv[z] = g_own[...]

    for peer in line:
        remote(g_own, g_recv.at[z], 8, (peer, f)).start()
    finish(g_recv.at[pl.ds(0, zs - 1)], 8)
    drain(id_buf.at[pl.ds(0, zs - 1)], 0)
    drain(w_recv.at[pl.ds(0, (m - 1) * slice_w)], 1)
    drain(mod_recv.at[pl.ds(0, m - 1)], 2)
    drain(row_recv.at[pl.ds(0, zs - 1)], 3)
    drain(tok_recv.at[0, pl.ds(0, chips - 1)], 4)
    drain(tok_recv.at[0], 12)
    drain(part_recv.at[pl.ds(0, ns - 1)], 5)
    drain(late_recv.at[pl.ds(0, ns - 1)], 6)
    drain(dkv_recv.at[pl.ds(0, ns - 1)], 7)
    drain(g_recv.at[pl.ds(0, zs - 1)], 8)
    drain(c_recv.at[pl.ds(0, ns - 1)], 9)
    drain(lab_recv.at[pl.ds(0, ns - 1)], 10)
    drain(idz_recv.at[pl.ds(0, zs - 1)], 11)


def owner_kernel(g_recv, belongs_a, belongs_b, meta, out):
    zs = g_recv.shape[0]
    half_n = g_recv.shape[1] * 2 // 3
    quarter = half_n // 2
    rows_own = meta.shape[1]
    own_scale = meta[...]

    wide = g_recv[...].astype(F32)
    sum_a = lax.dot_general(
        wide[:, :half_n, :].reshape(zs * half_n, LANES).astype(BF),
        belongs_a[...],
        TN_DIMS,
        preferred_element_type=F32,
    )
    sum_b = lax.dot_general(
        wide[:, half_n:, :].reshape(zs * quarter, LANES).astype(BF),
        belongs_b[...],
        TN_DIMS,
        preferred_element_type=F32,
    )
    top_rows = sum_a[:64, :rows_own] + sum_a[64:, rows_own:]
    low_rows = sum_b[:32, :rows_own]
    for c in range(1, 4):
        low_rows += sum_b[c * 32 : c * 32 + 32, c * rows_own : (c + 1) * rows_own]
    out[:64, :] = top_rows * own_scale
    out[64:, :] = low_rows * own_scale


def shards(
    txt_tokens,
    concept_table,
    concept_ids,
    positions,
    timesteps,
    counts,
    mod_table,
    kv_weight,
    kv_bias,
    key_gain,
    img_query,
    img_key,
    img_value,
    out_grad,
):
    ns = lax.axis_size("fsdp")
    zs = lax.axis_size("dp")
    nx, ny = (4, 4) if ns == 32 else (2, 2)
    m = ny * 2
    tok_len, width = txt_tokens.shape[1:]
    slice_w, kv_w = kv_weight.shape
    head_w = kv_w // 2
    heads = head_w // LANES
    n_img = img_query.shape[1]
    buckets = mod_table.shape[0]
    rows_own = concept_table.shape[0]
    block = kv_w // m
    group_w = slice_w * m
    n_c = width // LANES
    slot = (2 * heads + 4 + 15) // 16 * 16

    vm = pl.BlockSpec(memory_space=pltpu.VMEM)
    sm = pl.BlockSpec(memory_space=pltpu.SMEM)
    hb = pl.BlockSpec(memory_space=pl.ANY)
    image = pltpu.VMEM((n_img, head_w), BF)
    stat = pltpu.VMEM((heads, 1, n_img), F32)
    outs = pl.pallas_call(
        functools.partial(step_kernel, (zs, nx, ny)),
        out_shape=(
            pltpu.VMEM((zs, ns * 3 // 4, LANES), BF),
            pltpu.VMEM((zs * ns // 2, 2 * rows_own), BF),
            pltpu.VMEM((zs * ns // 4, 4 * rows_own), BF),
            pltpu.VMEM((1, rows_own), F32),
        ),
        in_specs=[sm] * 3 + [hb] * 11,
        out_specs=(vm,) * 4,
        scratch_shapes=[
            pltpu.VMEM((tok_len, width), BF),
            pltpu.VMEM((1, rows_own), jnp.int32),
            pltpu.VMEM((buckets, 2, slice_w), BF),
            pltpu.VMEM((1, kv_w), F32),
            pltpu.VMEM((1, LANES), F32),
            pltpu.VMEM((rows_own, width), BF),
            pltpu.VMEM((slice_w, kv_w), BF),
            image,
            image,
            image,
            image,
            pltpu.VMEM((buckets, 2, LANES), F32),
            pltpu.VMEM((2 * buckets, LANES), BF),
            pltpu.VMEM((1, LANES), F32),
            pltpu.VMEM((ns, 1, LANES), F32),
            pltpu.VMEM((1, LANES), F32),
            pltpu.VMEM((zs, 1, LANES), F32),
            pltpu.VMEM((zs, 1, LANES), jnp.int32),
            pltpu.VMEM((1, LANES), jnp.int32),
            pltpu.VMEM((zs, n_c, LANES), F32),
            pltpu.VMEM((zs, n_c, LANES), BF),
            pltpu.VMEM((zs, n_c, LANES), BF),
            pltpu.VMEM((n_c, LANES), F32),
            pltpu.VMEM((1, width), F32),
            pltpu.VMEM((ny, tok_len, nx * slice_w), F32),
            pltpu.VMEM((nx, tok_len, ny * slice_w), F32),
            pltpu.VMEM((nx * ny, tok_len, group_w), BF),
            pltpu.VMEM((2, nx * ny, tok_len, group_w), BF),
            pltpu.VMEM((nx * ny, 1, group_w), F32),
            pltpu.VMEM((ns, 1, group_w), F32),
            pltpu.VMEM((kv_w, slice_w), BF),
            pltpu.VMEM((group_w, block), BF),
            pltpu.VMEM((m, 2 * buckets, LANES), BF),
            pltpu.VMEM((ns, tok_len, block), F32),
            pltpu.VMEM((ns, tok_len, block), F32),
            pltpu.VMEM((ns, 2, block), F32),
            pltpu.VMEM((ns, 2, block), F32),
            pltpu.VMEM((tok_len, kv_w), F32),
            stat,
            stat,
            stat,
            pltpu.VMEM((slot, LANES), F32),
            pltpu.VMEM((heads, LANES), F32),
            pltpu.VMEM((2 * heads, LANES), F32),
            pltpu.VMEM((2 * heads, LANES), F32),
            pltpu.VMEM((slot, LANES), BF),
            pltpu.VMEM((ns, slot, LANES), BF),
            pltpu.VMEM((ns, slot, LANES), F32),
            pltpu.VMEM((ns * 3 // 4, LANES), F32),
            pltpu.VMEM((ns * 3 // 4, LANES), BF),
            pltpu.SemaphoreType.DMA((11,)),
            pltpu.SemaphoreType.DMA((13,)),
            pltpu.SemaphoreType.DMA((13,)),
        ],
        compiler_params=pltpu.CompilerParams(collective_id=0, has_side_effects=True),
    )(
        concept_ids,
        positions,
        timesteps,
        txt_tokens[0],
        counts[None, :],
        mod_table,
        kv_bias[None, :],
        key_gain[None, :],
        concept_table,
        kv_weight,
        img_query[0],
        img_key[0],
        img_value[0],
        out_grad[0],
    )
    grad_t = pl.pallas_call(
        owner_kernel,
        out_shape=jax.ShapeDtypeStruct((slice_w, rows_own), F32),
        in_specs=[vm] * 4,
        out_specs=vm,
    )(*(pltpu.with_memory_space_constraint(o, pltpu.VMEM) for o in outs))
    return grad_t.T


def solution(mesh):
    placed = (
        P(("dp", "fsdp"), None, None),
        P("dp", None),
        P(("dp", "fsdp")),
        P(("dp", "fsdp")),
        P(("dp", "fsdp")),
        P("dp"),
        P(None, None, "fsdp"),
        P("fsdp", None),
        P(),
        P(),
        P(("dp", "fsdp"), None, None),
        P(("dp", "fsdp"), None, None),
        P(("dp", "fsdp"), None, None),
        P(("dp", "fsdp"), None, None),
    )
    return jax.shard_map(
        shards, mesh=mesh, in_specs=placed, out_specs=P("dp", "fsdp"), check_vma=False
    )
```

```python
import functools
import jax
import jax.numpy as jnp
from jax import lax
from jax.experimental import pallas as pl
from jax.experimental.pallas import tpu as pltpu
from jax.sharding import PartitionSpec as P

EPSILON = 1e-06
LANES = 128
BF = jnp.bfloat16
F32 = jnp.float32
MESH = pl.DeviceIdType.MESH
NT_DIMS = (((1,), (1,)), ((), ()))
TN_DIMS = (((0,), (0,)), ((), ()))


def split_two(values):
    high = values.astype(BF)
    low = (values - high.astype(F32)).astype(BF)
    return high, low


def iota(shape, axis):
    return lax.broadcasted_iota(jnp.int32, shape, axis)


def far_first(sizes):
    steps = [(a, b, c) for a in range(sizes[0]) for b in range(sizes[1]) for c in range(2)]

    def hops(step):
        return sum(min(d, n - d) for d, n in zip(step[:2], sizes))

    return sorted(steps[1:], key=lambda step: (-hops(step), step))


def step_kernel(
    dims,
    ids_s,
    pos_s,
    time_s,
    tok_any,
    counts_any,
    mods_any,
    bias_any,
    gain_any,
    table_any,
    weight_any,
    q_any,
    k_any,
    v_any,
    g_any,
    g_recv,
    belongs_a,
    belongs_b,
    meta,
    tok,
    counts,
    mods,
    bias,
    gain,
    table,
    weight,
    q,
    k,
    v,
    g,
    mod32,
    modp,
    lab_own,
    lab_recv,
    idz_own,
    idz_recv,
    id_buf,
    id_own,
    row32,
    row_send,
    row_recv,
    c32,
    c_row,
    cut_a,
    cut_b,
    tok_msg,
    tok_recv,
    c_msg,
    c_recv,
    w_t,
    w_recv,
    mod_recv,
    part,
    part_recv,
    late,
    late_recv,
    kv,
    m_img,
    l_img,
    d_img,
    m_rest,
    l_rest,
    d_rest,
    dkv32,
    raw32,
    s1_32,
    s2_32,
    dkv_own,
    mean_own,
    mean_recv,
    dkv_recv,
    dkv_wide,
    g32,
    g_own,
    load_sem,
    send_sem,
    recv_sem,
):
    zs, nx, ny = dims
    ns = nx * ny * 2
    m = ny * 2
    z = lax.axis_index("dp")
    f = lax.axis_index("fsdp")
    groups = nx
    my_x = lax.div(f, m)
    my_y = lax.div(lax.rem(f, m), 2)
    my_c = lax.rem(f, 2)
    tok_len, width = tok.shape
    slice_w = weight.shape[0]
    kv_w = weight.shape[1]
    head_w = kv_w // 2
    heads = head_w // LANES
    block = kv_w // m
    group_w = slice_w * m
    n_img = q.shape[0]
    rows_own = table.shape[0]
    buckets = mods.shape[0]
    inv_root = 1.0 / (LANES**0.5)

    x_at = [lax.rem(my_x + d, nx) for d in range(nx)]
    y_at = [lax.rem(my_y + d, ny) for d in range(ny)]
    c_at = [my_c, 1 - my_c]
    chips = nx * ny
    plane = [
        ((x_at[a] * ny + y_at[b]) * 2 + c_at[c], c_at[c] * chips + x_at[a] * ny + y_at[b])
        for a, b, c in far_first((nx, ny))
    ]
    same_core = [
        ((x_at[a] * ny + y_at[b]) * 2 + my_c, x_at[a] * ny + y_at[b])
        for a, b, c in far_first((nx, ny))
        if c == 0
    ]
    chip_of = [x_at[a] * ny + y_at[b] for a, b, c in far_first((nx, ny))]
    me_chip = my_x * ny + my_y
    me = my_c * chips + me_chip
    from_me = my_x * m + lax.rem(my_x + my_y, ny) * 2 + my_c
    ring = my_x * (1 - my_c) + my_y * my_c
    own_slot = my_c * nx + ring
    own_block = lax.rem(my_x + my_y, ny) * 2 + my_c
    mates = []
    for b, c in sorted(
        ((b, c) for b in range(ny) for c in range(2)), key=lambda bc: -min(bc[0], ny - bc[0])
    ):
        if b or c:
            mate_x = lax.rem(my_x + b * (1 - my_c), nx)
            mate_y = lax.rem(my_y + b * my_c, ny)
            mates.append(
                (
                    (mate_x * ny + mate_y) * 2 + c_at[c],
                    lax.rem(mate_x + mate_y, ny) * 2 + c_at[c],
                )
            )
    line = [
        lax.rem(z + d, zs) for d in sorted(range(1, zs), key=lambda d: (-min(d, zs - d), d))
    ]

    barrier = pltpu.get_barrier_semaphore()
    for peer in line:
        pl.semaphore_signal(barrier, inc=1, device_id=(peer, f), device_id_type=MESH)

    pairs = (
        (tok_any, tok),
        (mods_any, mods),
        (weight_any, weight),
        (q_any, q),
        (k_any, k),
        (v_any, v),
        (g_any, g),
        (table_any, table),
        (counts_any, counts),
        (bias_any, bias),
        (gain_any, gain),
    )
    loads = [
        pltpu.make_async_copy(src, dst, load_sem.at[i]) for i, (src, dst) in enumerate(pairs)
    ]
    for copy in loads:
        copy.start()

    for peer, _ in plane:
        pl.semaphore_signal(barrier, inc=1, device_id=(z, peer), device_id_type=MESH)

    own_id = ids_s[0]
    own_pos = pos_s[0]
    own_time = time_s[0]
    id_own[...] = jnp.full(id_own.shape, own_id, jnp.int32)
    id_buf[z] = id_own[...]

    lane = iota((1, LANES), 1)
    label = jnp.where(lane == 0, own_time, jnp.where(lane == 1, own_pos, own_id))
    lab_own[...] = label.astype(F32)
    lab_recv[me] = lab_own[...]
    at_pos = iota((tok_len, 1), 0) == own_pos

    loads[0].wait()
    tok_f = tok[...].astype(F32)
    centre = jnp.mean(tok_f, -1, keepdims=True)
    spread = jnp.mean((tok_f - centre) ** 2, -1, keepdims=True)
    tok_hat = ((tok_f - centre) * lax.rsqrt(spread + EPSILON)).astype(BF)
    half_w = nx * slice_w
    tok_32 = tok_hat.astype(F32)
    for a in range(nx):
        for b in range(ny):
            at = (a * ny + b) * 2 * slice_w
            cut_a[b, :, a * slice_w : (a + 1) * slice_w] = tok_32[:, at : at + slice_w]
            at += slice_w
            cut_b[a, :, b * slice_w : (b + 1) * slice_w] = tok_32[:, at : at + slice_w]
    for a in range(nx):
        for b in range(ny):
            tok_msg[a * ny + b, :, :half_w] = cut_a[b].astype(BF)
            tok_msg[a * ny + b, :, half_w:] = cut_b[a].astype(BF)
    tok_recv[my_c, me_chip] = tok_msg[me_chip]

    mod32[...] = jnp.zeros(mod32.shape, F32)
    loads[1].wait()
    mod32[:, :, :slice_w] = mods[...].astype(F32)
    modp[:buckets, :] = mod32[:, 0, :].astype(BF)
    modp[buckets:, :] = mod32[:, 1, :].astype(BF)
    mod_recv[own_slot] = modp[...]
    loads[2].wait()
    w_recv[pl.ds(pl.multiple_of(own_slot * slice_w, 16), slice_w), :] = weight[
        :, pl.ds(pl.multiple_of(own_block * block, LANES), block)
    ]

    pl.semaphore_wait(barrier, zs - 1 + ns - 1)

    def remote(src, dst, phase, device):
        return pltpu.make_async_remote_copy(
            src_ref=src,
            dst_ref=dst,
            send_sem=send_sem.at[phase],
            recv_sem=recv_sem.at[phase],
            device_id=device,
            device_id_type=MESH,
        )

    def finish(ref, phase):
        pltpu.make_async_copy(ref, ref, recv_sem.at[phase]).wait()

    def drain(ref, phase):
        pltpu.make_async_copy(ref, ref, send_sem.at[phase]).wait()

    for peer in line:
        remote(id_own, id_buf.at[z], 0, (peer, f)).start()

    for peer, _ in plane:
        remote(lab_own, lab_recv.at[me], 10, (z, peer)).start()

    for peer, chip in same_core:
        remote(tok_msg.at[chip], tok_recv.at[my_c, me_chip], 4, (z, peer)).start()

    for peer, _ in mates:
        remote(modp, mod_recv.at[own_slot], 2, (z, peer)).start()

    for peer, theirs in mates:
        remote(
            weight.at[:, pl.ds(pl.multiple_of(theirs * block, LANES), block)],
            w_recv.at[pl.ds(pl.multiple_of(own_slot * slice_w, 16), slice_w), :],
            1,
            (z, peer),
        ).start()

    for copy in loads[3:]:
        copy.wait()

    def image_head(h, c):
        lanes = pl.ds(pl.multiple_of(h * LANES, LANES), LANES)
        scores = (
            lax.dot_general(k[:, lanes], q[:, lanes], NT_DIMS, preferred_element_type=F32)
            * inv_root
        )
        grads = lax.dot_general(v[:, lanes], g[:, lanes], NT_DIMS, preferred_element_type=F32)
        top = jnp.max(scores, 0, keepdims=True)
        raised = jnp.exp(scores - top)
        m_img[h] = top
        l_img[h] = jnp.sum(raised, 0, keepdims=True)
        d_img[h] = jnp.sum(raised.astype(BF).astype(F32) * grads, 0, keepdims=True)
        return c

    half = heads // 4
    lax.fori_loop(0, half, image_head, 0)

    table_f = table[...].astype(F32)
    t_centre = jnp.mean(table_f, -1, keepdims=True)
    t_spread = jnp.mean((table_f - t_centre) ** 2, -1, keepdims=True)
    t_rstd = lax.rsqrt(t_spread + EPSILON)
    table[...] = ((table_f - t_centre) * t_rstd).astype(BF)
    diag = iota((rows_own, rows_own), 0) == iota((rows_own, rows_own), 1)
    meta[...] = jnp.sum(jnp.where(diag, t_rstd, 0.0), 0, keepdims=True) / counts[...].astype(F32)

    finish(id_buf.at[pl.ds(0, zs - 1)], 0)
    wanted = id_buf[:, 0, :][:, :1]
    pick = (iota((zs, rows_own), 1) + z * rows_own == wanted).astype(F32).astype(BF)
    rows = jnp.dot(pick, table[...], preferred_element_type=F32)
    for c in range(width // LANES):
        row32[:, c, :] = rows[:, c * LANES : (c + 1) * LANES]
    row_send[...] = row32[...].astype(BF)
    row_recv[z] = row_send[z]
    for peer in line:
        remote(row_send.at[peer], row_recv.at[z], 3, (peer, f)).start()

    finish(lab_recv.at[pl.ds(0, ns - 1)], 10)
    labels = lab_recv[:, 0, :]
    pick_s = (iota((ns, buckets), 1) == labels[:, 0:1].astype(jnp.int32)).astype(F32).astype(BF)
    scale_own = 1.0 + jnp.dot(pick_s, modp[buckets:, :], preferred_element_type=F32)

    sample_diag = iota((ns, LANES), 0) == iota((ns, LANES), 1)
    idz_own[...] = jnp.sum(jnp.where(sample_diag, labels[:, 2:3], 0.0), 0, keepdims=True)
    idz_recv[z] = idz_own[...]
    for peer in line:
        remote(idz_own, idz_recv.at[z], 11, (peer, f)).start()

    finish(tok_recv.at[0, pl.ds(0, chips - 1)], 4)
    remote(tok_recv.at[my_c], tok_recv.at[my_c], 12, (z, f + 1 - 2 * my_c)).start()

    finish(mod_recv.at[pl.ds(0, m - 1)], 2)
    lane_row = iota((LANES, group_w), 0)
    lane_col = iota((LANES, group_w), 1)
    mod_sum = jnp.zeros((2 * buckets, group_w), F32)
    for c in range(m):
        place = ((lane_col == lane_row + c * slice_w) & (lane_row < slice_w)).astype(F32)
        mod_sum += jnp.dot(mod_recv[c], place.astype(BF), preferred_element_type=F32)
    shift_s = jnp.dot(pick_s, mod_sum[:buckets].astype(BF), preferred_element_type=F32)
    scale_s = 1.0 + jnp.dot(pick_s, mod_sum[buckets:].astype(BF), preferred_element_type=F32)

    finish(tok_recv.at[0], 12)
    toks = tok_recv[...].astype(F32).reshape(ns, tok_len, group_w)
    modulated = scale_s.reshape(ns, 1, group_w) * toks + shift_s.reshape(ns, 1, group_w)
    a_high, a_low = split_two(scale_s)
    placed = iota((ns, tok_len, 1), 1) == lab_recv[:, :, 1:2].astype(jnp.int32)
    finish(w_recv.at[pl.ds(0, (m - 1) * slice_w)], 1)
    terms = jnp.dot(
        modulated.reshape(ns * tok_len, group_w).astype(BF),
        w_recv[...],
        preferred_element_type=F32,
    )
    extra = jnp.dot(
        jnp.concatenate([a_high, a_low], 0), w_recv[...], preferred_element_type=F32
    )
    sums = (extra[:ns] + extra[ns:]).reshape(ns, 1, block)
    part[...] = jnp.where(placed, sums, terms.reshape(ns, tok_len, block))
    part_recv[from_me] = part[me]
    for peer, slot in plane:
        remote(part.at[slot], part_recv.at[from_me], 5, (z, peer)).start()

    lax.fori_loop(half, heads, image_head, 0)

    finish(row_recv.at[pl.ds(0, zs - 1)], 3)
    concept = jnp.sum(row_recv[...].astype(F32), 0)
    c32[...] = concept
    for c in range(width // LANES):
        c_row[:, c * LANES : (c + 1) * LANES] = c32[c : c + 1, :]
    for a in range(nx):
        for b in range(ny):
            at = (a * ny + b) * 2 * slice_w
            cut_a[b, 0:1, a * slice_w : (a + 1) * slice_w] = c_row[:, at : at + slice_w]
            at += slice_w
            cut_b[a, 0:1, b * slice_w : (b + 1) * slice_w] = c_row[:, at : at + slice_w]
    for a in range(nx):
        for b in range(ny):
            c_msg[a * ny + b, :, :half_w] = cut_a[b, 0:1, :]
            c_msg[a * ny + b, :, half_w:] = cut_b[a, 0:1, :]
    c_recv[me] = c_msg[me_chip]
    for (peer, _), chip in zip(plane, chip_of):
        remote(c_msg.at[chip], c_recv.at[me], 9, (z, peer)).start()

    own_row = iota((group_w, LANES), 0)
    own_col = iota((group_w, LANES), 1)
    own_place = ((own_row == own_col + own_slot * slice_w) & (own_col < slice_w)).astype(F32).astype(BF)

    finish(c_recv.at[pl.ds(0, ns - 1)], 9)
    concepts = c_recv[:, 0, :]
    scaled = scale_s * concepts
    b_high, b_low = split_two(scaled)
    extra = jnp.dot(
        jnp.concatenate([(scaled + shift_s).astype(BF), b_high, b_low], 0),
        w_recv[...],
        preferred_element_type=F32,
    )
    late[:, 0, :] = extra[:ns]
    late[:, 1, :] = extra[ns : 2 * ns] + extra[2 * ns :]
    late_recv[from_me] = late[me]
    for peer, slot in plane:
        remote(late.at[slot], late_recv.at[from_me], 6, (z, peer)).start()
    concept_own = jnp.dot(concepts.astype(BF), own_place, preferred_element_type=F32)

    finish(idz_recv.at[pl.ds(0, zs - 1)], 11)
    half_n, quarter = ns // 2, ns // 4
    id_cols = jnp.sum(
        jnp.where(sample_diag.reshape(1, ns, LANES), idz_recv[...], 0.0), -1, keepdims=True
    ).astype(jnp.int32)
    belongs = (iota((zs, ns, rows_own), 2) + z * rows_own == id_cols).astype(F32)
    for c in range(2):
        belongs_a[:, c * rows_own : (c + 1) * rows_own] = (
            belongs[:, c * half_n : (c + 1) * half_n, :].reshape(zs * half_n, rows_own).astype(BF)
        )
    for c in range(4):
        belongs_b[:, c * rows_own : (c + 1) * rows_own] = (
            belongs[:, c * quarter : (c + 1) * quarter, :]
            .reshape(zs * quarter, rows_own)
            .astype(BF)
        )

    for c in range(2 * heads):
        lanes = slice(c * LANES, (c + 1) * LANES)
        w_t[lanes, :] = weight[:, lanes].astype(F32).T.astype(BF)

    finish(part_recv.at[pl.ds(0, ns - 1)], 5)
    per = block // LANES
    pos_f = at_pos.astype(F32)
    for c in range(m):
        total = part_recv[c]
        for a in range(1, groups):
            total += part_recv[a * m + c]
        first = jnp.sum(total * pos_f, 0, keepdims=True)
        kv[:, c * block : (c + 1) * block] = total + bias[:, c * block : (c + 1) * block]
        for b in range(per):
            s1_32[c * per + b : c * per + b + 1, :] = first[:, b * LANES : (b + 1) * LANES]
    kv_all = kv[...]
    gains = gain[...]
    key_parts = []
    for h in range(heads):
        raw = kv_all[:, h * LANES : (h + 1) * LANES]
        inv = lax.rsqrt(jnp.mean(raw * raw, -1, keepdims=True) + EPSILON)
        key_parts.append((raw * inv * gains).astype(BF).astype(F32))
    key_txt = jnp.concatenate(key_parts, 1)
    val_txt = kv_all[:, head_w:].astype(BF).astype(F32)
    own_head = iota((heads * tok_len, head_w), 0) // tok_len == iota(
        (heads * tok_len, head_w), 1
    ) // LANES
    key_diag = jnp.where(own_head, jnp.concatenate([key_txt] * heads, 0), 0.0).astype(BF)
    val_diag = jnp.where(own_head, jnp.concatenate([val_txt] * heads, 0), 0.0).astype(BF)
    s_txt = (
        lax.dot_general(key_diag, q[...], NT_DIMS, preferred_element_type=F32) * inv_root
    ).reshape(heads, tok_len, n_img)
    g_txt = lax.dot_general(val_diag, g[...], NT_DIMS, preferred_element_type=F32).reshape(
        heads, tok_len, n_img
    )
    other = iota((1, tok_len, 1), 1) != own_pos
    top_img = m_img[...]
    top = jnp.maximum(top_img, jnp.max(jnp.where(other, s_txt, -3e38), 1, keepdims=True))
    raised = jnp.where(other, jnp.exp(jnp.where(other, s_txt, top) - top), 0.0)
    alpha = jnp.exp(top_img - top)
    m_rest[...] = top[:, 0, :]
    l_rest[...] = (alpha * l_img[...] + jnp.sum(raised, 1, keepdims=True))[:, 0, :]
    d_rest[...] = (
        alpha * d_img[...] + jnp.sum(raised.astype(BF).astype(F32) * g_txt, 1, keepdims=True)
    )[:, 0, :]

    finish(late_recv.at[pl.ds(0, ns - 1)], 6)
    for c in range(m):
        extras = late_recv[c]
        for a in range(1, groups):
            extras += late_recv[a * m + c]
        raw_row = extras[0:1, :] + bias[:, c * block : (c + 1) * block]
        for b in range(per):
            lanes = slice(b * LANES, (b + 1) * LANES)
            raw32[c * per + b : c * per + b + 1, :] = raw_row[:, lanes]
            s2_32[c * per + b : c * per + b + 1, :] = extras[1:2, lanes]
    raw_pos = raw32[:heads, :]
    inv_pos = lax.rsqrt(jnp.mean(raw_pos * raw_pos, -1, keepdims=True) + EPSILON)
    key_pos = (raw_pos * inv_pos * gains).astype(BF).astype(F32)
    val_pos = raw32[heads:, :].astype(BF).astype(F32)
    own_lane = iota((heads, head_w), 0) == iota((heads, head_w), 1) // LANES
    key_diag = jnp.where(own_lane, jnp.concatenate([key_pos] * heads, 1), 0.0).astype(BF)
    val_diag = jnp.where(own_lane, jnp.concatenate([val_pos] * heads, 1), 0.0).astype(BF)
    s_pos = lax.dot_general(key_diag, q[...], NT_DIMS, preferred_element_type=F32) * inv_root
    g_pos = lax.dot_general(val_diag, g[...], NT_DIMS, preferred_element_type=F32)
    top_rest = m_rest[...]
    top = jnp.maximum(top_rest, s_pos)
    raised = jnp.exp(s_pos - top)
    alpha = jnp.exp(top_rest - top)
    denom = alpha * l_rest[...] + raised
    p_pos = raised / denom
    delta = alpha * d_rest[...] / denom + p_pos.astype(BF).astype(F32) * g_pos
    d_score = p_pos * (g_pos - delta) * inv_root
    p_high, p_low = split_two(p_pos)
    d_high, d_low = split_two(d_score)
    d_val = jnp.dot(
        jnp.concatenate([p_high.astype(F32), p_low.astype(F32)], 0).astype(BF),
        g[...],
        preferred_element_type=F32,
    )
    d_key = jnp.dot(
        jnp.concatenate([d_high.astype(F32), d_low.astype(F32)], 0).astype(BF),
        q[...],
        preferred_element_type=F32,
    )
    d_val = d_val[:heads] + d_val[heads:]
    d_key = d_key[:heads] + d_key[heads:]
    for h in range(heads):
        dkv32[h : h + 1, :] = d_key[h : h + 1, h * LANES : (h + 1) * LANES]
        dkv32[heads + h : heads + h + 1, :] = d_val[h : h + 1, h * LANES : (h + 1) * LANES]
    n_pos = raw_pos * inv_pos
    d_norm = dkv32[:heads, :] * gains
    dkv32[:heads, :] = inv_pos * (d_norm - n_pos * jnp.mean(d_norm * n_pos, -1, keepdims=True))
    dkv_own[...] = dkv32[...].astype(BF)
    dkv_recv[me] = dkv_own[...]

    dkv_rows = dkv_own[...].astype(F32)
    mean_own[0:1, :] = jnp.sum(dkv_rows * s1_32[...], 0, keepdims=True)
    mean_own[1:2, :] = jnp.sum(dkv_rows * s2_32[...], 0, keepdims=True)
    mean_recv[me] = mean_own[...]
    for peer, _ in plane:
        remote(mean_own, mean_recv.at[me], 13, (z, peer)).start()
        remote(dkv_own, dkv_recv.at[me], 7, (z, peer)).start()
    finish(mean_recv.at[pl.ds(0, ns - 1)], 13)
    finish(dkv_recv.at[pl.ds(0, ns - 1)], 7)
    dkv_wide[...] = dkv_recv[...].astype(F32)
    grads = jnp.zeros((ns, slice_w), F32)
    for c in range(0, 2 * heads, 2):
        both = jnp.concatenate([dkv_wide[:, c, :], dkv_wide[:, c + 1, :]], 1).astype(BF)
        grads += jnp.dot(
            both, w_t[c * LANES : (c + 2) * LANES, :], preferred_element_type=F32
        )
    mean_1 = jnp.sum(mean_recv[:, 0, :], -1, keepdims=True) / width
    mean_2 = jnp.sum(mean_recv[:, 1, :], -1, keepdims=True) / width
    row_grad = grads * scale_own[:, :slice_w] - mean_1 - concept_own[:, :slice_w] * mean_2
    for c in range(2):
        g32[:half_n, c * 64 : c * 64 + 64] = row_grad[c * half_n : (c + 1) * half_n, :64]
    for c in range(4):
        g32[half_n:, c * 32 : c * 32 + 32] = row_grad[c * quarter : (c + 1) * quarter, 64:]
    g_own[...] = g32[...].astype(BF)
    g_recv[z] = g_own[...]

    for peer in line:
        remote(g_own, g_recv.at[z], 8, (peer, f)).start()
    finish(g_recv.at[pl.ds(0, zs - 1)], 8)
    drain(id_buf.at[pl.ds(0, zs - 1)], 0)
    drain(w_recv.at[pl.ds(0, (m - 1) * slice_w)], 1)
    drain(mod_recv.at[pl.ds(0, m - 1)], 2)
    drain(row_recv.at[pl.ds(0, zs - 1)], 3)
    drain(tok_recv.at[0, pl.ds(0, chips - 1)], 4)
    drain(tok_recv.at[0], 12)
    drain(part_recv.at[pl.ds(0, ns - 1)], 5)
    drain(late_recv.at[pl.ds(0, ns - 1)], 6)
    drain(dkv_recv.at[pl.ds(0, ns - 1)], 7)
    drain(g_recv.at[pl.ds(0, zs - 1)], 8)
    drain(c_recv.at[pl.ds(0, ns - 1)], 9)
    drain(lab_recv.at[pl.ds(0, ns - 1)], 10)
    drain(idz_recv.at[pl.ds(0, zs - 1)], 11)
    drain(mean_recv.at[pl.ds(0, ns - 1)], 13)


def owner_kernel(g_recv, belongs_a, belongs_b, meta, out):
    zs = g_recv.shape[0]
    half_n = g_recv.shape[1] * 2 // 3
    quarter = half_n // 2
    rows_own = meta.shape[1]
    own_scale = meta[...]

    wide = g_recv[...].astype(F32)
    sum_a = lax.dot_general(
        wide[:, :half_n, :].reshape(zs * half_n, LANES).astype(BF),
        belongs_a[...],
        TN_DIMS,
        preferred_element_type=F32,
    )
    sum_b = lax.dot_general(
        wide[:, half_n:, :].reshape(zs * quarter, LANES).astype(BF),
        belongs_b[...],
        TN_DIMS,
        preferred_element_type=F32,
    )
    top_rows = sum_a[:64, :rows_own] + sum_a[64:, rows_own:]
    low_rows = sum_b[:32, :rows_own]
    for c in range(1, 4):
        low_rows += sum_b[c * 32 : c * 32 + 32, c * rows_own : (c + 1) * rows_own]
    out[:64, :] = top_rows * own_scale
    out[64:, :] = low_rows * own_scale


def shards(
    txt_tokens,
    concept_table,
    concept_ids,
    positions,
    timesteps,
    counts,
    mod_table,
    kv_weight,
    kv_bias,
    key_gain,
    img_query,
    img_key,
    img_value,
    out_grad,
):
    ns = lax.axis_size("fsdp")
    zs = lax.axis_size("dp")
    nx, ny = (4, 4) if ns == 32 else (2, 2)
    m = ny * 2
    tok_len, width = txt_tokens.shape[1:]
    slice_w, kv_w = kv_weight.shape
    head_w = kv_w // 2
    heads = head_w // LANES
    n_img = img_query.shape[1]
    buckets = mod_table.shape[0]
    rows_own = concept_table.shape[0]
    block = kv_w // m
    group_w = slice_w * m
    n_c = width // LANES
    slot = 2 * heads

    vm = pl.BlockSpec(memory_space=pltpu.VMEM)
    sm = pl.BlockSpec(memory_space=pltpu.SMEM)
    hb = pl.BlockSpec(memory_space=pl.ANY)
    image = pltpu.VMEM((n_img, head_w), BF)
    stat = pltpu.VMEM((heads, 1, n_img), F32)
    outs = pl.pallas_call(
        functools.partial(step_kernel, (zs, nx, ny)),
        out_shape=(
            pltpu.VMEM((zs, ns * 3 // 4, LANES), BF),
            pltpu.VMEM((zs * ns // 2, 2 * rows_own), BF),
            pltpu.VMEM((zs * ns // 4, 4 * rows_own), BF),
            pltpu.VMEM((1, rows_own), F32),
        ),
        in_specs=[sm] * 3 + [hb] * 11,
        out_specs=(vm,) * 4,
        scratch_shapes=[
            pltpu.VMEM((tok_len, width), BF),
            pltpu.VMEM((1, rows_own), jnp.int32),
            pltpu.VMEM((buckets, 2, slice_w), BF),
            pltpu.VMEM((1, kv_w), F32),
            pltpu.VMEM((1, LANES), F32),
            pltpu.VMEM((rows_own, width), BF),
            pltpu.VMEM((slice_w, kv_w), BF),
            image,
            image,
            image,
            image,
            pltpu.VMEM((buckets, 2, LANES), F32),
            pltpu.VMEM((2 * buckets, LANES), BF),
            pltpu.VMEM((1, LANES), F32),
            pltpu.VMEM((ns, 1, LANES), F32),
            pltpu.VMEM((1, LANES), F32),
            pltpu.VMEM((zs, 1, LANES), F32),
            pltpu.VMEM((zs, 1, LANES), jnp.int32),
            pltpu.VMEM((1, LANES), jnp.int32),
            pltpu.VMEM((zs, n_c, LANES), F32),
            pltpu.VMEM((zs, n_c, LANES), BF),
            pltpu.VMEM((zs, n_c, LANES), BF),
            pltpu.VMEM((n_c, LANES), F32),
            pltpu.VMEM((1, width), F32),
            pltpu.VMEM((ny, tok_len, nx * slice_w), F32),
            pltpu.VMEM((nx, tok_len, ny * slice_w), F32),
            pltpu.VMEM((nx * ny, tok_len, group_w), BF),
            pltpu.VMEM((2, nx * ny, tok_len, group_w), BF),
            pltpu.VMEM((nx * ny, 1, group_w), F32),
            pltpu.VMEM((ns, 1, group_w), F32),
            pltpu.VMEM((kv_w, slice_w), BF),
            pltpu.VMEM((group_w, block), BF),
            pltpu.VMEM((m, 2 * buckets, LANES), BF),
            pltpu.VMEM((ns, tok_len, block), F32),
            pltpu.VMEM((ns, tok_len, block), F32),
            pltpu.VMEM((ns, 2, block), F32),
            pltpu.VMEM((ns, 2, block), F32),
            pltpu.VMEM((tok_len, kv_w), F32),
            stat,
            stat,
            stat,
            pltpu.VMEM((heads, n_img), F32),
            pltpu.VMEM((heads, n_img), F32),
            pltpu.VMEM((heads, n_img), F32),
            pltpu.VMEM((slot, LANES), F32),
            pltpu.VMEM((2 * heads, LANES), F32),
            pltpu.VMEM((2 * heads, LANES), F32),
            pltpu.VMEM((2 * heads, LANES), F32),
            pltpu.VMEM((slot, LANES), BF),
            pltpu.VMEM((2, LANES), F32),
            pltpu.VMEM((ns, 2, LANES), F32),
            pltpu.VMEM((ns, slot, LANES), BF),
            pltpu.VMEM((ns, slot, LANES), F32),
            pltpu.VMEM((ns * 3 // 4, LANES), F32),
            pltpu.VMEM((ns * 3 // 4, LANES), BF),
            pltpu.SemaphoreType.DMA((11,)),
            pltpu.SemaphoreType.DMA((14,)),
            pltpu.SemaphoreType.DMA((14,)),
        ],
        compiler_params=pltpu.CompilerParams(collective_id=0, has_side_effects=True),
    )(
        concept_ids,
        positions,
        timesteps,
        txt_tokens[0],
        counts[None, :],
        mod_table,
        kv_bias[None, :],
        key_gain[None, :],
        concept_table,
        kv_weight,
        img_query[0],
        img_key[0],
        img_value[0],
        out_grad[0],
    )
    grad_t = pl.pallas_call(
        owner_kernel,
        out_shape=jax.ShapeDtypeStruct((slice_w, rows_own), F32),
        in_specs=[vm] * 4,
        out_specs=vm,
    )(*(pltpu.with_memory_space_constraint(o, pltpu.VMEM) for o in outs))
    return grad_t.T


def solution(mesh):
    placed = (
        P(("dp", "fsdp"), None, None),
        P("dp", None),
        P(("dp", "fsdp")),
        P(("dp", "fsdp")),
        P(("dp", "fsdp")),
        P("dp"),
        P(None, None, "fsdp"),
        P("fsdp", None),
        P(),
        P(),
        P(("dp", "fsdp"), None, None),
        P(("dp", "fsdp"), None, None),
        P(("dp", "fsdp"), None, None),
        P(("dp", "fsdp"), None, None),
    )
    return jax.shard_map(
        shards, mesh=mesh, in_specs=placed, out_specs=P("dp", "fsdp"), check_vma=False
    )
```

```python
import functools
import jax
import jax.numpy as jnp
from jax import lax
from jax.experimental import pallas as pl
from jax.experimental.pallas import tpu as pltpu
from jax.sharding import PartitionSpec as P

EPSILON = 1e-06
LANES = 128
BF = jnp.bfloat16
F32 = jnp.float32
MESH = pl.DeviceIdType.MESH
NT_DIMS = (((1,), (1,)), ((), ()))
TN_DIMS = (((0,), (0,)), ((), ()))


def split_two(values):
    high = values.astype(BF)
    low = (values - high.astype(F32)).astype(BF)
    return high, low


def iota(shape, axis):
    return lax.broadcasted_iota(jnp.int32, shape, axis)


def far_first(sizes):
    steps = [(a, b, c) for a in range(sizes[0]) for b in range(sizes[1]) for c in range(2)]

    def hops(step):
        return sum(min(d, n - d) for d, n in zip(step[:2], sizes))

    return sorted(steps[1:], key=lambda step: (-hops(step), step))


def step_kernel(
    dims,
    ids_s,
    pos_s,
    time_s,
    tok_any,
    counts_any,
    mods_any,
    bias_any,
    gain_any,
    table_any,
    weight_any,
    q_any,
    k_any,
    v_any,
    g_any,
    g_recv,
    belongs_a,
    belongs_b,
    meta,
    tok,
    counts,
    mods,
    bias,
    gain,
    table,
    weight,
    q,
    k,
    v,
    g,
    mod32,
    modp,
    lab_own,
    lab_recv,
    idz_own,
    idz_recv,
    id_buf,
    id_own,
    row32,
    row_send,
    row_recv,
    c32,
    c_row,
    cut_a,
    cut_b,
    tok_msg,
    tok_recv,
    c_msg,
    c_recv,
    w_t,
    w_recv,
    mod_recv,
    part,
    part_recv,
    late,
    late_recv,
    kv,
    m_img,
    l_img,
    d_img,
    m_rest,
    l_rest,
    d_rest,
    dkv32,
    raw32,
    s1_32,
    s2_32,
    dkv_own,
    mean_own,
    mean_recv,
    dkv_recv,
    dkv_wide,
    g32,
    g_own,
    load_sem,
    send_sem,
    recv_sem,
):
    zs, nx, ny = dims
    ns = nx * ny * 2
    m = ny * 2
    z = lax.axis_index("dp")
    f = lax.axis_index("fsdp")
    groups = nx
    my_x = lax.div(f, m)
    my_y = lax.div(lax.rem(f, m), 2)
    my_c = lax.rem(f, 2)
    tok_len, width = tok.shape
    slice_w = weight.shape[0]
    kv_w = weight.shape[1]
    head_w = kv_w // 2
    heads = head_w // LANES
    block = kv_w // m
    group_w = slice_w * m
    n_img = q.shape[0]
    rows_own = table.shape[0]
    buckets = mods.shape[0]
    inv_root = 1.0 / (LANES**0.5)

    x_at = [lax.rem(my_x + d, nx) for d in range(nx)]
    y_at = [lax.rem(my_y + d, ny) for d in range(ny)]
    c_at = [my_c, 1 - my_c]
    chips = nx * ny
    plane = [
        ((x_at[a] * ny + y_at[b]) * 2 + c_at[c], c_at[c] * chips + x_at[a] * ny + y_at[b])
        for a, b, c in far_first((nx, ny))
    ]
    same_core = [
        ((x_at[a] * ny + y_at[b]) * 2 + my_c, x_at[a] * ny + y_at[b])
        for a, b, c in far_first((nx, ny))
        if c == 0
    ]
    chip_of = [x_at[a] * ny + y_at[b] for a, b, c in far_first((nx, ny))]
    me_chip = my_x * ny + my_y
    me = my_c * chips + me_chip
    from_me = my_x * m + lax.rem(my_x + my_y, ny) * 2 + my_c
    ring = my_x * (1 - my_c) + my_y * my_c
    own_slot = my_c * nx + ring
    own_block = lax.rem(my_x + my_y, ny) * 2 + my_c
    mates = []
    same_ring = []
    for b, c in sorted(
        ((b, c) for b in range(ny) for c in range(2)), key=lambda bc: -min(bc[0], ny - bc[0])
    ):
        if b or c:
            mate_x = lax.rem(my_x + b * (1 - my_c), nx)
            mate_y = lax.rem(my_y + b * my_c, ny)
            if c == 0:
                same_ring.append((mate_x * ny + mate_y) * 2 + my_c)
            mates.append(
                (
                    (mate_x * ny + mate_y) * 2 + c_at[c],
                    lax.rem(mate_x + mate_y, ny) * 2 + c_at[c],
                )
            )
    line = [
        lax.rem(z + d, zs) for d in sorted(range(1, zs), key=lambda d: (-min(d, zs - d), d))
    ]

    barrier = pltpu.get_barrier_semaphore()
    for peer in line:
        pl.semaphore_signal(barrier, inc=1, device_id=(peer, f), device_id_type=MESH)

    pairs = (
        (tok_any, tok),
        (mods_any, mods),
        (weight_any, weight),
        (q_any, q),
        (k_any, k),
        (v_any, v),
        (g_any, g),
        (table_any, table),
        (counts_any, counts),
        (bias_any, bias),
        (gain_any, gain),
    )
    loads = [
        pltpu.make_async_copy(src, dst, load_sem.at[i]) for i, (src, dst) in enumerate(pairs)
    ]
    for copy in loads:
        copy.start()

    for peer, _ in plane:
        pl.semaphore_signal(barrier, inc=1, device_id=(z, peer), device_id_type=MESH)

    own_id = ids_s[0]
    own_pos = pos_s[0]
    own_time = time_s[0]
    id_own[...] = jnp.full(id_own.shape, own_id, jnp.int32)
    id_buf[z] = id_own[...]

    lane = iota((1, LANES), 1)
    label = jnp.where(lane == 0, own_time, jnp.where(lane == 1, own_pos, own_id))
    lab_own[...] = label.astype(F32)
    lab_recv[me] = lab_own[...]
    at_pos = iota((tok_len, 1), 0) == own_pos

    loads[0].wait()
    tok_f = tok[...].astype(F32)
    centre = jnp.mean(tok_f, -1, keepdims=True)
    spread = jnp.mean((tok_f - centre) ** 2, -1, keepdims=True)
    tok_hat = ((tok_f - centre) * lax.rsqrt(spread + EPSILON)).astype(BF)
    half_w = nx * slice_w
    tok_32 = tok_hat.astype(F32)
    for a in range(nx):
        for b in range(ny):
            at = (a * ny + b) * 2 * slice_w
            cut_a[b, :, a * slice_w : (a + 1) * slice_w] = tok_32[:, at : at + slice_w]
            at += slice_w
            cut_b[a, :, b * slice_w : (b + 1) * slice_w] = tok_32[:, at : at + slice_w]
    for a in range(nx):
        for b in range(ny):
            tok_msg[a * ny + b, :, :half_w] = cut_a[b].astype(BF)
            tok_msg[a * ny + b, :, half_w:] = cut_b[a].astype(BF)
    tok_recv[my_c, me_chip] = tok_msg[me_chip]

    mod32[...] = jnp.zeros(mod32.shape, F32)
    loads[1].wait()
    mod32[:, :, :slice_w] = mods[...].astype(F32)
    modp[:buckets, :] = mod32[:, 0, :].astype(BF)
    modp[buckets:, :] = mod32[:, 1, :].astype(BF)
    mod_recv[own_slot] = modp[...]
    loads[2].wait()
    w_recv[pl.ds(pl.multiple_of(own_slot * slice_w, 16), slice_w), :] = weight[
        :, pl.ds(pl.multiple_of(own_block * block, LANES), block)
    ]

    pl.semaphore_wait(barrier, zs - 1 + ns - 1)

    def remote(src, dst, phase, device):
        return pltpu.make_async_remote_copy(
            src_ref=src,
            dst_ref=dst,
            send_sem=send_sem.at[phase],
            recv_sem=recv_sem.at[phase],
            device_id=device,
            device_id_type=MESH,
        )

    def finish(ref, phase):
        pltpu.make_async_copy(ref, ref, recv_sem.at[phase]).wait()

    def drain(ref, phase):
        pltpu.make_async_copy(ref, ref, send_sem.at[phase]).wait()

    for peer in line:
        remote(id_own, id_buf.at[z], 0, (peer, f)).start()

    for peer, _ in plane:
        remote(lab_own, lab_recv.at[me], 10, (z, peer)).start()

    for peer in same_ring:
        remote(modp, mod_recv.at[own_slot], 2, (z, peer)).start()

    for peer, theirs in mates:
        remote(
            weight.at[:, pl.ds(pl.multiple_of(theirs * block, LANES), block)],
            w_recv.at[pl.ds(pl.multiple_of(own_slot * slice_w, 16), slice_w), :],
            1,
            (z, peer),
        ).start()

    for peer, chip in same_core:
        remote(tok_msg.at[chip], tok_recv.at[my_c, me_chip], 4, (z, peer)).start()

    for copy in loads[3:]:
        copy.wait()

    def image_head(h, c):
        lanes = pl.ds(pl.multiple_of(h * LANES, LANES), LANES)
        scores = (
            lax.dot_general(k[:, lanes], q[:, lanes], NT_DIMS, preferred_element_type=F32)
            * inv_root
        )
        grads = lax.dot_general(v[:, lanes], g[:, lanes], NT_DIMS, preferred_element_type=F32)
        top = jnp.max(scores, 0, keepdims=True)
        raised = jnp.exp(scores - top)
        m_img[h] = top
        l_img[h] = jnp.sum(raised, 0, keepdims=True)
        d_img[h] = jnp.sum(raised.astype(BF).astype(F32) * grads, 0, keepdims=True)
        return c

    half = heads // 4
    lax.fori_loop(0, half, image_head, 0)

    table_f = table[...].astype(F32)
    t_centre = jnp.mean(table_f, -1, keepdims=True)
    t_spread = jnp.mean((table_f - t_centre) ** 2, -1, keepdims=True)
    t_rstd = lax.rsqrt(t_spread + EPSILON)
    table[...] = ((table_f - t_centre) * t_rstd).astype(BF)
    diag = iota((rows_own, rows_own), 0) == iota((rows_own, rows_own), 1)
    meta[...] = jnp.sum(jnp.where(diag, t_rstd, 0.0), 0, keepdims=True) / counts[...].astype(F32)

    finish(id_buf.at[pl.ds(0, zs - 1)], 0)
    wanted = id_buf[:, 0, :][:, :1]
    pick = (iota((zs, rows_own), 1) + z * rows_own == wanted).astype(F32).astype(BF)
    rows = jnp.dot(pick, table[...], preferred_element_type=F32)
    for c in range(width // LANES):
        row32[:, c, :] = rows[:, c * LANES : (c + 1) * LANES]
    row_send[...] = row32[...].astype(BF)
    row_recv[z] = row_send[z]
    for peer in line:
        remote(row_send.at[peer], row_recv.at[z], 3, (peer, f)).start()

    finish(lab_recv.at[pl.ds(0, ns - 1)], 10)
    labels = lab_recv[:, 0, :]
    pick_s = (iota((ns, buckets), 1) == labels[:, 0:1].astype(jnp.int32)).astype(F32).astype(BF)
    scale_own = 1.0 + jnp.dot(pick_s, modp[buckets:, :], preferred_element_type=F32)

    sample_diag = iota((ns, LANES), 0) == iota((ns, LANES), 1)
    idz_own[...] = jnp.sum(jnp.where(sample_diag, labels[:, 2:3], 0.0), 0, keepdims=True)
    idz_recv[z] = idz_own[...]
    for peer in line:
        remote(idz_own, idz_recv.at[z], 11, (peer, f)).start()

    ring_slots = mod_recv.at[pl.ds(my_c * nx, nx)]
    finish(mod_recv.at[pl.ds(0, nx - 1)], 2)
    remote(ring_slots, ring_slots, 14, (z, f + 1 - 2 * my_c)).start()

    finish(tok_recv.at[0, pl.ds(0, chips - 1)], 4)
    remote(tok_recv.at[my_c], tok_recv.at[my_c], 12, (z, f + 1 - 2 * my_c)).start()

    finish(mod_recv.at[pl.ds(0, nx)], 14)
    lane_row = iota((LANES, group_w), 0)
    lane_col = iota((LANES, group_w), 1)
    mod_sum = jnp.zeros((2 * buckets, group_w), F32)
    for c in range(m):
        place = ((lane_col == lane_row + c * slice_w) & (lane_row < slice_w)).astype(F32)
        mod_sum += jnp.dot(mod_recv[c], place.astype(BF), preferred_element_type=F32)
    shift_s = jnp.dot(pick_s, mod_sum[:buckets].astype(BF), preferred_element_type=F32)
    scale_s = 1.0 + jnp.dot(pick_s, mod_sum[buckets:].astype(BF), preferred_element_type=F32)

    finish(tok_recv.at[0], 12)
    toks = tok_recv[...].astype(F32).reshape(ns, tok_len, group_w)
    modulated = scale_s.reshape(ns, 1, group_w) * toks + shift_s.reshape(ns, 1, group_w)
    a_high, a_low = split_two(scale_s)
    placed = iota((ns, tok_len, 1), 1) == lab_recv[:, :, 1:2].astype(jnp.int32)
    finish(w_recv.at[pl.ds(0, (m - 1) * slice_w)], 1)
    terms = jnp.dot(
        modulated.reshape(ns * tok_len, group_w).astype(BF),
        w_recv[...],
        preferred_element_type=F32,
    )
    extra = jnp.dot(
        jnp.concatenate([a_high, a_low], 0), w_recv[...], preferred_element_type=F32
    )
    sums = (extra[:ns] + extra[ns:]).reshape(ns, 1, block)
    part[...] = jnp.where(placed, sums, terms.reshape(ns, tok_len, block))
    part_recv[from_me] = part[me]
    for peer, slot in plane:
        remote(part.at[slot], part_recv.at[from_me], 5, (z, peer)).start()

    lax.fori_loop(half, heads, image_head, 0)

    finish(row_recv.at[pl.ds(0, zs - 1)], 3)
    concept = jnp.sum(row_recv[...].astype(F32), 0)
    c32[...] = concept
    for c in range(width // LANES):
        c_row[:, c * LANES : (c + 1) * LANES] = c32[c : c + 1, :]
    for a in range(nx):
        for b in range(ny):
            at = (a * ny + b) * 2 * slice_w
            cut_a[b, 0:1, a * slice_w : (a + 1) * slice_w] = c_row[:, at : at + slice_w]
            at += slice_w
            cut_b[a, 0:1, b * slice_w : (b + 1) * slice_w] = c_row[:, at : at + slice_w]
    for a in range(nx):
        for b in range(ny):
            c_msg[a * ny + b, :, :half_w] = cut_a[b, 0:1, :]
            c_msg[a * ny + b, :, half_w:] = cut_b[a, 0:1, :]
    c_recv[me] = c_msg[me_chip]
    for (peer, _), chip in zip(plane, chip_of):
        remote(c_msg.at[chip], c_recv.at[me], 9, (z, peer)).start()

    own_row = iota((group_w, LANES), 0)
    own_col = iota((group_w, LANES), 1)
    own_place = ((own_row == own_col + own_slot * slice_w) & (own_col < slice_w)).astype(F32).astype(BF)

    finish(c_recv.at[pl.ds(0, ns - 1)], 9)
    concepts = c_recv[:, 0, :]
    scaled = scale_s * concepts
    b_high, b_low = split_two(scaled)
    extra = jnp.dot(
        jnp.concatenate([(scaled + shift_s).astype(BF), b_high, b_low], 0),
        w_recv[...],
        preferred_element_type=F32,
    )
    late[:, 0, :] = extra[:ns]
    late[:, 1, :] = extra[ns : 2 * ns] + extra[2 * ns :]
    late_recv[from_me] = late[me]
    for peer, slot in plane:
        remote(late.at[slot], late_recv.at[from_me], 6, (z, peer)).start()
    concept_own = jnp.dot(concepts.astype(BF), own_place, preferred_element_type=F32)

    finish(idz_recv.at[pl.ds(0, zs - 1)], 11)
    half_n, quarter = ns // 2, ns // 4
    id_cols = jnp.sum(
        jnp.where(sample_diag.reshape(1, ns, LANES), idz_recv[...], 0.0), -1, keepdims=True
    ).astype(jnp.int32)
    belongs = (iota((zs, ns, rows_own), 2) + z * rows_own == id_cols).astype(F32)
    for c in range(2):
        belongs_a[:, c * rows_own : (c + 1) * rows_own] = (
            belongs[:, c * half_n : (c + 1) * half_n, :].reshape(zs * half_n, rows_own).astype(BF)
        )
    for c in range(4):
        belongs_b[:, c * rows_own : (c + 1) * rows_own] = (
            belongs[:, c * quarter : (c + 1) * quarter, :]
            .reshape(zs * quarter, rows_own)
            .astype(BF)
        )

    for c in range(2 * heads):
        lanes = slice(c * LANES, (c + 1) * LANES)
        w_t[lanes, :] = weight[:, lanes].astype(F32).T.astype(BF)

    finish(part_recv.at[pl.ds(0, ns - 1)], 5)
    per = block // LANES
    pos_f = at_pos.astype(F32)
    for c in range(m):
        total = part_recv[c]
        for a in range(1, groups):
            total += part_recv[a * m + c]
        first = jnp.sum(total * pos_f, 0, keepdims=True)
        kv[:, c * block : (c + 1) * block] = total + bias[:, c * block : (c + 1) * block]
        for b in range(per):
            s1_32[c * per + b : c * per + b + 1, :] = first[:, b * LANES : (b + 1) * LANES]
    kv_all = kv[...]
    gains = gain[...]
    key_parts = []
    for h in range(heads):
        raw = kv_all[:, h * LANES : (h + 1) * LANES]
        inv = lax.rsqrt(jnp.mean(raw * raw, -1, keepdims=True) + EPSILON)
        key_parts.append((raw * inv * gains).astype(BF).astype(F32))
    key_txt = jnp.concatenate(key_parts, 1)
    val_txt = kv_all[:, head_w:].astype(BF).astype(F32)
    own_head = iota((heads * tok_len, head_w), 0) // tok_len == iota(
        (heads * tok_len, head_w), 1
    ) // LANES
    key_diag = jnp.where(own_head, jnp.concatenate([key_txt] * heads, 0), 0.0).astype(BF)
    val_diag = jnp.where(own_head, jnp.concatenate([val_txt] * heads, 0), 0.0).astype(BF)
    s_txt = (
        lax.dot_general(key_diag, q[...], NT_DIMS, preferred_element_type=F32) * inv_root
    ).reshape(heads, tok_len, n_img)
    g_txt = lax.dot_general(val_diag, g[...], NT_DIMS, preferred_element_type=F32).reshape(
        heads, tok_len, n_img
    )
    other = iota((1, tok_len, 1), 1) != own_pos
    top_img = m_img[...]
    top = jnp.maximum(top_img, jnp.max(jnp.where(other, s_txt, -3e38), 1, keepdims=True))
    raised = jnp.where(other, jnp.exp(jnp.where(other, s_txt, top) - top), 0.0)
    alpha = jnp.exp(top_img - top)
    m_rest[...] = top[:, 0, :]
    l_rest[...] = (alpha * l_img[...] + jnp.sum(raised, 1, keepdims=True))[:, 0, :]
    d_rest[...] = (
        alpha * d_img[...] + jnp.sum(raised.astype(BF).astype(F32) * g_txt, 1, keepdims=True)
    )[:, 0, :]

    finish(late_recv.at[pl.ds(0, ns - 1)], 6)
    for c in range(m):
        extras = late_recv[c]
        for a in range(1, groups):
            extras += late_recv[a * m + c]
        raw_row = extras[0:1, :] + bias[:, c * block : (c + 1) * block]
        for b in range(per):
            lanes = slice(b * LANES, (b + 1) * LANES)
            raw32[c * per + b : c * per + b + 1, :] = raw_row[:, lanes]
            s2_32[c * per + b : c * per + b + 1, :] = extras[1:2, lanes]
    raw_pos = raw32[:heads, :]
    inv_pos = lax.rsqrt(jnp.mean(raw_pos * raw_pos, -1, keepdims=True) + EPSILON)
    key_pos = (raw_pos * inv_pos * gains).astype(BF).astype(F32)
    val_pos = raw32[heads:, :].astype(BF).astype(F32)
    own_lane = iota((heads, head_w), 0) == iota((heads, head_w), 1) // LANES
    key_diag = jnp.where(own_lane, jnp.concatenate([key_pos] * heads, 1), 0.0).astype(BF)
    val_diag = jnp.where(own_lane, jnp.concatenate([val_pos] * heads, 1), 0.0).astype(BF)
    s_pos = lax.dot_general(key_diag, q[...], NT_DIMS, preferred_element_type=F32) * inv_root
    g_pos = lax.dot_general(val_diag, g[...], NT_DIMS, preferred_element_type=F32)
    top_rest = m_rest[...]
    top = jnp.maximum(top_rest, s_pos)
    raised = jnp.exp(s_pos - top)
    alpha = jnp.exp(top_rest - top)
    denom = alpha * l_rest[...] + raised
    p_pos = raised / denom
    delta = alpha * d_rest[...] / denom + p_pos.astype(BF).astype(F32) * g_pos
    d_score = p_pos * (g_pos - delta) * inv_root
    p_high, p_low = split_two(p_pos)
    d_high, d_low = split_two(d_score)
    d_val = jnp.dot(
        jnp.concatenate([p_high.astype(F32), p_low.astype(F32)], 0).astype(BF),
        g[...],
        preferred_element_type=F32,
    )
    d_key = jnp.dot(
        jnp.concatenate([d_high.astype(F32), d_low.astype(F32)], 0).astype(BF),
        q[...],
        preferred_element_type=F32,
    )
    d_val = d_val[:heads] + d_val[heads:]
    d_key = d_key[:heads] + d_key[heads:]
    for h in range(heads):
        dkv32[h : h + 1, :] = d_key[h : h + 1, h * LANES : (h + 1) * LANES]
        dkv32[heads + h : heads + h + 1, :] = d_val[h : h + 1, h * LANES : (h + 1) * LANES]
    n_pos = raw_pos * inv_pos
    d_norm = dkv32[:heads, :] * gains
    dkv32[:heads, :] = inv_pos * (d_norm - n_pos * jnp.mean(d_norm * n_pos, -1, keepdims=True))
    dkv_own[...] = dkv32[...].astype(BF)
    dkv_recv[me] = dkv_own[...]

    dkv_rows = dkv_own[...].astype(F32)
    mean_own[0:1, :] = jnp.sum(dkv_rows * s1_32[...], 0, keepdims=True)
    mean_own[1:2, :] = jnp.sum(dkv_rows * s2_32[...], 0, keepdims=True)
    mean_recv[me] = mean_own[...]
    for peer, _ in plane:
        remote(mean_own, mean_recv.at[me], 13, (z, peer)).start()
        remote(dkv_own, dkv_recv.at[me], 7, (z, peer)).start()
    finish(mean_recv.at[pl.ds(0, ns - 1)], 13)
    finish(dkv_recv.at[pl.ds(0, ns - 1)], 7)
    dkv_wide[...] = dkv_recv[...].astype(F32)
    grads = jnp.zeros((ns, slice_w), F32)
    for c in range(0, 2 * heads, 2):
        both = jnp.concatenate([dkv_wide[:, c, :], dkv_wide[:, c + 1, :]], 1).astype(BF)
        grads += jnp.dot(
            both, w_t[c * LANES : (c + 2) * LANES, :], preferred_element_type=F32
        )
    mean_1 = jnp.sum(mean_recv[:, 0, :], -1, keepdims=True) / width
    mean_2 = jnp.sum(mean_recv[:, 1, :], -1, keepdims=True) / width
    row_grad = grads * scale_own[:, :slice_w] - mean_1 - concept_own[:, :slice_w] * mean_2
    for c in range(2):
        g32[:half_n, c * 64 : c * 64 + 64] = row_grad[c * half_n : (c + 1) * half_n, :64]
    for c in range(4):
        g32[half_n:, c * 32 : c * 32 + 32] = row_grad[c * quarter : (c + 1) * quarter, 64:]
    g_own[...] = g32[...].astype(BF)
    g_recv[z] = g_own[...]

    for peer in line:
        remote(g_own, g_recv.at[z], 8, (peer, f)).start()
    finish(g_recv.at[pl.ds(0, zs - 1)], 8)
    drain(id_buf.at[pl.ds(0, zs - 1)], 0)
    drain(w_recv.at[pl.ds(0, (m - 1) * slice_w)], 1)
    drain(mod_recv.at[pl.ds(0, nx - 1)], 2)
    drain(mod_recv.at[pl.ds(0, nx)], 14)
    drain(row_recv.at[pl.ds(0, zs - 1)], 3)
    drain(tok_recv.at[0, pl.ds(0, chips - 1)], 4)
    drain(tok_recv.at[0], 12)
    drain(part_recv.at[pl.ds(0, ns - 1)], 5)
    drain(late_recv.at[pl.ds(0, ns - 1)], 6)
    drain(dkv_recv.at[pl.ds(0, ns - 1)], 7)
    drain(g_recv.at[pl.ds(0, zs - 1)], 8)
    drain(c_recv.at[pl.ds(0, ns - 1)], 9)
    drain(lab_recv.at[pl.ds(0, ns - 1)], 10)
    drain(idz_recv.at[pl.ds(0, zs - 1)], 11)
    drain(mean_recv.at[pl.ds(0, ns - 1)], 13)


def owner_kernel(g_recv, belongs_a, belongs_b, meta, out):
    zs = g_recv.shape[0]
    half_n = g_recv.shape[1] * 2 // 3
    quarter = half_n // 2
    rows_own = meta.shape[1]
    own_scale = meta[...]

    wide = g_recv[...].astype(F32)
    sum_a = lax.dot_general(
        wide[:, :half_n, :].reshape(zs * half_n, LANES).astype(BF),
        belongs_a[...],
        TN_DIMS,
        preferred_element_type=F32,
    )
    sum_b = lax.dot_general(
        wide[:, half_n:, :].reshape(zs * quarter, LANES).astype(BF),
        belongs_b[...],
        TN_DIMS,
        preferred_element_type=F32,
    )
    top_rows = sum_a[:64, :rows_own] + sum_a[64:, rows_own:]
    low_rows = sum_b[:32, :rows_own]
    for c in range(1, 4):
        low_rows += sum_b[c * 32 : c * 32 + 32, c * rows_own : (c + 1) * rows_own]
    out[:64, :] = top_rows * own_scale
    out[64:, :] = low_rows * own_scale


def shards(
    txt_tokens,
    concept_table,
    concept_ids,
    positions,
    timesteps,
    counts,
    mod_table,
    kv_weight,
    kv_bias,
    key_gain,
    img_query,
    img_key,
    img_value,
    out_grad,
):
    ns = lax.axis_size("fsdp")
    zs = lax.axis_size("dp")
    nx, ny = (4, 4) if ns == 32 else (2, 2)
    m = ny * 2
    tok_len, width = txt_tokens.shape[1:]
    slice_w, kv_w = kv_weight.shape
    head_w = kv_w // 2
    heads = head_w // LANES
    n_img = img_query.shape[1]
    buckets = mod_table.shape[0]
    rows_own = concept_table.shape[0]
    block = kv_w // m
    group_w = slice_w * m
    n_c = width // LANES
    slot = 2 * heads

    vm = pl.BlockSpec(memory_space=pltpu.VMEM)
    sm = pl.BlockSpec(memory_space=pltpu.SMEM)
    hb = pl.BlockSpec(memory_space=pl.ANY)
    image = pltpu.VMEM((n_img, head_w), BF)
    stat = pltpu.VMEM((heads, 1, n_img), F32)
    outs = pl.pallas_call(
        functools.partial(step_kernel, (zs, nx, ny)),
        out_shape=(
            pltpu.VMEM((zs, ns * 3 // 4, LANES), BF),
            pltpu.VMEM((zs * ns // 2, 2 * rows_own), BF),
            pltpu.VMEM((zs * ns // 4, 4 * rows_own), BF),
            pltpu.VMEM((1, rows_own), F32),
        ),
        in_specs=[sm] * 3 + [hb] * 11,
        out_specs=(vm,) * 4,
        scratch_shapes=[
            pltpu.VMEM((tok_len, width), BF),
            pltpu.VMEM((1, rows_own), jnp.int32),
            pltpu.VMEM((buckets, 2, slice_w), BF),
            pltpu.VMEM((1, kv_w), F32),
            pltpu.VMEM((1, LANES), F32),
            pltpu.VMEM((rows_own, width), BF),
            pltpu.VMEM((slice_w, kv_w), BF),
            image,
            image,
            image,
            image,
            pltpu.VMEM((buckets, 2, LANES), F32),
            pltpu.VMEM((2 * buckets, LANES), BF),
            pltpu.VMEM((1, LANES), F32),
            pltpu.VMEM((ns, 1, LANES), F32),
            pltpu.VMEM((1, LANES), F32),
            pltpu.VMEM((zs, 1, LANES), F32),
            pltpu.VMEM((zs, 1, LANES), jnp.int32),
            pltpu.VMEM((1, LANES), jnp.int32),
            pltpu.VMEM((zs, n_c, LANES), F32),
            pltpu.VMEM((zs, n_c, LANES), BF),
            pltpu.VMEM((zs, n_c, LANES), BF),
            pltpu.VMEM((n_c, LANES), F32),
            pltpu.VMEM((1, width), F32),
            pltpu.VMEM((ny, tok_len, nx * slice_w), F32),
            pltpu.VMEM((nx, tok_len, ny * slice_w), F32),
            pltpu.VMEM((nx * ny, tok_len, group_w), BF),
            pltpu.VMEM((2, nx * ny, tok_len, group_w), BF),
            pltpu.VMEM((nx * ny, 1, group_w), F32),
            pltpu.VMEM((ns, 1, group_w), F32),
            pltpu.VMEM((kv_w, slice_w), BF),
            pltpu.VMEM((group_w, block), BF),
            pltpu.VMEM((m, 2 * buckets, LANES), BF),
            pltpu.VMEM((ns, tok_len, block), F32),
            pltpu.VMEM((ns, tok_len, block), F32),
            pltpu.VMEM((ns, 2, block), F32),
            pltpu.VMEM((ns, 2, block), F32),
            pltpu.VMEM((tok_len, kv_w), F32),
            stat,
            stat,
            stat,
            pltpu.VMEM((heads, n_img), F32),
            pltpu.VMEM((heads, n_img), F32),
            pltpu.VMEM((heads, n_img), F32),
            pltpu.VMEM((slot, LANES), F32),
            pltpu.VMEM((2 * heads, LANES), F32),
            pltpu.VMEM((2 * heads, LANES), F32),
            pltpu.VMEM((2 * heads, LANES), F32),
            pltpu.VMEM((slot, LANES), BF),
            pltpu.VMEM((2, LANES), F32),
            pltpu.VMEM((ns, 2, LANES), F32),
            pltpu.VMEM((ns, slot, LANES), BF),
            pltpu.VMEM((ns, slot, LANES), F32),
            pltpu.VMEM((ns * 3 // 4, LANES), F32),
            pltpu.VMEM((ns * 3 // 4, LANES), BF),
            pltpu.SemaphoreType.DMA((11,)),
            pltpu.SemaphoreType.DMA((15,)),
            pltpu.SemaphoreType.DMA((15,)),
        ],
        compiler_params=pltpu.CompilerParams(collective_id=0, has_side_effects=True),
    )(
        concept_ids,
        positions,
        timesteps,
        txt_tokens[0],
        counts[None, :],
        mod_table,
        kv_bias[None, :],
        key_gain[None, :],
        concept_table,
        kv_weight,
        img_query[0],
        img_key[0],
        img_value[0],
        out_grad[0],
    )
    grad_t = pl.pallas_call(
        owner_kernel,
        out_shape=jax.ShapeDtypeStruct((slice_w, rows_own), F32),
        in_specs=[vm] * 4,
        out_specs=vm,
    )(*(pltpu.with_memory_space_constraint(o, pltpu.VMEM) for o in outs))
    return grad_t.T


def solution(mesh):
    placed = (
        P(("dp", "fsdp"), None, None),
        P("dp", None),
        P(("dp", "fsdp")),
        P(("dp", "fsdp")),
        P(("dp", "fsdp")),
        P("dp"),
        P(None, None, "fsdp"),
        P("fsdp", None),
        P(),
        P(),
        P(("dp", "fsdp"), None, None),
        P(("dp", "fsdp"), None, None),
        P(("dp", "fsdp"), None, None),
        P(("dp", "fsdp"), None, None),
    )
    return jax.shard_map(
        shards, mesh=mesh, in_specs=placed, out_specs=P("dp", "fsdp"), check_vma=False
    )
```
